32 devices in a mesh: groups: 2 (over x), branch: 16 (over z, y, core).
Axes of the slice: x: 2, y: 2, z: 4, core: 2. Of those that a mesh axis runs over, the one named last changes fastest.
Arguments:
- prompt_k: bfloat16 [32, 1024, 1024], P(('groups', 'branch')), parts along dimension 0, may hold values from -6 to 6
- prompt_v: bfloat16 [32, 1024, 1024], P(('groups', 'branch')), parts along dimension 0, may hold values from -6 to 6
- prompt_mask: int32 [32, 8], P(('groups', 'branch')), parts along dimension 0, may hold values from 0 to 1, as said below
- shared_kv: bfloat16 [64, 24, 2048], P(('groups', 'branch')), parts along dimension 0, may hold values from -6 to 6
- shared_len: int32 [64], P(('groups', 'branch')), parts along dimension 0, may hold values from 1 to 24, 400 in all
- send_pick: int32 [32, 16], P(('groups', 'branch')), parts along dimension 0, may hold values from -1 to 1, as said below
- unique_q: bfloat16 [512, 8192], P(('groups', 'branch')), parts along dimension 0, may hold values from -132 to 132
- unique_kv: bfloat16 [512, 2048], P(('groups', 'branch')), parts along dimension 0, may hold values from -6.5 to 6.5
- unique_owner: int32 [512, 1], P(('groups', 'branch')), parts along dimension 0, may hold values from 0 to 15; in each aligned block of 16 rows (0 to 15, 16 to 31, ...) at most 2 rows name the same one
Outputs:
- attended: bfloat16 [512, 8192], P(('groups', 'branch')), parts along dimension 0
The draws below stay inside these ranges and needn't reach their ends.
There are 2 independent parts, one for each index of `groups`. The reference program is written for one: setup_inputs(seed, part) draws one part's arguments, and reference() takes and returns one part's arrays. A program takes and returns all parts, laid end to end along the dimension named above; each array names one. Nothing has to cross between parts.
Inputs may be any that keep to these rules, and one draw needn't show every extreme that they name: `prompt_mask`: block 0 of every branch's prompt is visible. `send_pick`: entry [s, b] names which of owner s's 2 results branch b subscribes to, or -1 for none; every branch subscribes to exactly 12 results, at most one of each owner. `unique_owner`: among the rows of one source, no branch is named by more than 2 rows.
All inputs are finite; a program needn't handle non-finite values. No bound on the sum of `shared_len` on one device may be relied on, other than what follows from the above.
Results may differ from the reference program's by a relative error of at most 0.0027.
Values may be sent and summed in bfloat16 or wider, within the bound.
A program may use at most 128 MiB of HBM per device.

```python
import math
import jax
import jax.numpy as jnp
import numpy as np
from jax import lax

QH = 64
KVH = 8
HD = 128
GRP = 8
QW = 8192
KVW = 1024
PLEN = 1024
PB = 128
PBLK = 8
RLEN = 24
RES_DEV = 2
NRES = 32
SUBS = 12
CAP = 2
UNQ_DEV = 16
ROWS = 256
N_BRANCH = 16


def draw_prompt_k(key, part):
    values = jnp.clip(jax.random.normal(jax.random.fold_in(key, 11), (N_BRANCH, PLEN, KVW), jnp.float32), -6.0, 6.0)
    return values.astype(jnp.bfloat16)


def draw_prompt_mask(key, part):
    levels = jax.random.randint(jax.random.fold_in(key, 19), (N_BRANCH, PBLK), 0, 4)
    visible = (levels > 0).astype(jnp.int32)
    return visible.at[:, 0].set(1)


def draw_send_pick(key, part):
    subkeys = jax.random.split(jax.random.fold_in(key, 23), N_BRANCH)
    ordering = jax.vmap(lambda single: jax.random.permutation(single, N_BRANCH))(subkeys)
    position = jnp.argsort(ordering, axis=1)
    which = jax.random.randint(jax.random.fold_in(key, 29), (N_BRANCH, N_BRANCH), 0, RES_DEV)
    picked = jnp.where(position < SUBS, which, -1)
    return picked.T.astype(jnp.int32)


def draw_unique_q(key, part):
    values = 3.0 * jnp.clip(jax.random.normal(jax.random.fold_in(key, 13), (ROWS, QW), jnp.float32), -6.0, 6.0)
    return values.astype(jnp.bfloat16)


def draw_unique_kv(key, part):
    values = jnp.clip(jax.random.normal(jax.random.fold_in(key, 17), (ROWS, 2 * KVW), jnp.float32), -6.0, 6.0)
    return values.astype(jnp.bfloat16)


def block_scale(stream_key, dims, cuts, least, top_value):
    level = 1.0
    for dim, shards_of in cuts:
        steps = jax.random.uniform(jax.random.fold_in(jax.random.fold_in(stream_key, 6), dim), (shards_of,), jnp.float32, least / len(cuts), top_value / len(cuts))
        level = level * jnp.repeat(jnp.exp(steps), dims[dim] // shards_of).reshape((-1,) + (1,) * (len(dims) - 1 - dim))
    return level


def split_up(amount, total, reach, skew):
    portions = [(1 << 20) // math.isqrt(rank ** skew) + 1 for rank in range(2, amount + 1)]
    surplus, counts = total - reach - (amount - 1), [1] * (amount - 1)
    while surplus > 0:
        candidates = [i for i in range(amount - 1) if counts[i] < reach]
        mass, budget = sum([portions[i] for i in candidates]), surplus
        for i in candidates:
            more = min(reach - counts[i], max(1, budget * portions[i] // mass), surplus)
            counts[i] = counts[i] + more
            surplus = surplus - more
    return np.array([reach] + counts)


def ragged_sizes(stream_key, number_of, total, most, slope):
    if number_of == 2:
        one = jax.random.randint(stream_key, (), max(1, total - most), min(most, total - 1) + 1)
        return jnp.stack([one, total - one])
    sizes = jnp.asarray(split_up(number_of, total, most, slope), jnp.int32)
    pairs = (number_of - 1) // 2
    source_of, sink = sizes[1:1 + 2 * pairs:2], sizes[2:2 + 2 * pairs:2]
    margin = jnp.minimum(source_of - 1, most - sink)
    shifted = jax.random.randint(jax.random.fold_in(stream_key, 1), (pairs,), 0, 1 << 20) % (margin + 1)
    sizes = sizes.at[1:1 + 2 * pairs:2].set(source_of - shifted).at[2:2 + 2 * pairs:2].set(sink + shifted)
    return sizes[jax.random.permutation(jax.random.fold_in(stream_key, 2), number_of)]


def shared_out(stream_key, own, number, rows, number_of, top, reach, lean):
    sequence = jax.random.permutation(stream_key, number_of)
    packed, ordinary = load_shares(number_of, rows * top, reach, lean, True), load_shares(number_of, rows * top, reach, lean, False)
    places = jnp.arange(number_of)

    def named(lengths, turn):
        used = int((lengths > 0).sum())
        fixed = max(1, used // 4)
        passed = fixed + (places - fixed + turn * (used - fixed)) % max(1, number_of - fixed)
        return jnp.zeros((number_of,), jnp.int32).at[sequence[jnp.where(places < fixed, places, passed)]].set(jnp.asarray(lengths, jnp.int32))

    lengths = jnp.where(number % 4 == 0, named(packed, number // 4), named(ordinary, number - number // 4 - 1))
    mixed = jax.random.permutation(jax.random.fold_in(own, 3), number_of)
    source_of, taker = mixed[0:number_of // 2 * 2:2], mixed[1:number_of // 2 * 2:2]
    slack = jnp.minimum(lengths[source_of] - 1, reach - lengths[taker]) // 2
    slack = jnp.where((source_of == sequence[0]) | (taker == sequence[0]) | (lengths[taker] == 0), 0, jnp.maximum(slack, 0))
    passed = jax.random.randint(jax.random.fold_in(own, 4), (number_of // 2,), 0, 1 << 20) % (slack + 1)
    lengths = lengths.at[source_of].add(-passed).at[taker].add(passed)
    labels = jnp.searchsorted(jnp.cumsum(lengths), jnp.arange(rows * top), side="right").astype(jnp.int32)
    grid = labels.reshape(top, rows).T
    grid = grid[jax.random.permutation(jax.random.fold_in(own, 1), rows)]
    turn = jax.random.randint(jax.random.fold_in(own, 2), (rows, 1), 0, top)
    return jnp.take_along_axis(grid, (jnp.arange(top)[None, :] + turn) % top, axis=1)


def load_shares(count, total, reach, lean, full):
    loads = [(1 << 20) // math.isqrt(rank ** lean) + 1 for rank in range(1, count + 1)]
    largest = reach if full else min(reach, max(-(-total // count), total * loads[0] // sum(loads)))
    least = 1 if total - largest >= count - 1 else 0
    counts, surplus = [largest] + [least] * (count - 1), total - largest - least * (count - 1)
    while surplus > 0:
        candidates = [i for i in range(1, count) if counts[i] < largest] or [i for i in range(1, count) if counts[i] < reach]
        mass, left = sum([loads[i] for i in candidates]), surplus
        for i in candidates:
            more = min(reach - counts[i], max(1, left * loads[i] // mass), surplus)
            counts[i] = counts[i] + more
            surplus = surplus - more
    return np.array(counts)


def normal_values(key, shape, scale, limit, pieces=(), held_as=jnp.bfloat16):
    array = jax.random.normal(key, shape, jnp.float32) * scale
    if len(pieces) > 0:
        array = block_scale(key, shape, pieces, -0.22, 0.18) * array
    return jnp.clip(array, min=-limit, max=limit).astype(held_as)


def setup_inputs(seed: int = 0, part: int = 0) -> dict:
    key_of = jax.random.split(jax.random.key(seed), 10)
    own_keys = jax.random.split(jax.random.fold_in(key_of[9], part), 10)
    prompt_k = draw_prompt_k(jax.random.fold_in(jax.random.fold_in(key_of[9], part), 71), part)
    prompt_v = normal_values(own_keys[1], (N_BRANCH, PLEN, KVW), 1.0, 6.0, ((0, 16),))
    prompt_mask = draw_prompt_mask(jax.random.fold_in(jax.random.fold_in(key_of[9], part), 71), part)
    shared_kv = normal_values(own_keys[3], (NRES, RLEN, 2 * KVW), 1.0, 6.0, ((0, 16),))
    shared_len = ragged_sizes(own_keys[4], NRES, NRES * (RLEN + 1) // 2, RLEN, 2).astype(jnp.int32)
    send_pick = draw_send_pick(jax.random.fold_in(jax.random.fold_in(key_of[9], part), 71), part)
    unique_q = draw_unique_q(jax.random.fold_in(jax.random.fold_in(key_of[9], part), 71), part)
    unique_kv = draw_unique_kv(jax.random.fold_in(jax.random.fold_in(key_of[9], part), 71), part)
    unique_owner_keys = jax.random.split(jax.random.fold_in(own_keys[8], 1), ROWS // UNQ_DEV)
    unique_owner_turns = jax.random.permutation(jax.random.fold_in(own_keys[8], 3), ROWS // UNQ_DEV)
    unique_owner = jax.vmap(lambda own, number: shared_out(jax.random.fold_in(own_keys[8], 2), own, number, UNQ_DEV, N_BRANCH, 1, CAP, 2))(unique_owner_keys, unique_owner_turns).reshape((ROWS, 1))
    return {"prompt_k": prompt_k, "prompt_v": prompt_v, "prompt_mask": prompt_mask, "shared_kv": shared_kv, "shared_len": shared_len, "send_pick": send_pick, "unique_q": unique_q, "unique_kv": unique_kv, "unique_owner": unique_owner}


def attend(queries, key_rows, value_rows, allowed):
    count = queries.shape[0]
    keys_total = key_rows.shape[0]
    grouped = queries.reshape(count, KVH, GRP, HD).transpose(1, 2, 0, 3).astype(jnp.float32)
    key_heads = key_rows.reshape(keys_total, KVH, HD).transpose(1, 0, 2).astype(jnp.float32)
    value_heads = value_rows.reshape(keys_total, KVH, HD).transpose(1, 0, 2).astype(jnp.float32)
    scale = 1.0 / math.sqrt(HD)

    def one_head(operands):
        query_group, key_group, value_group = operands
        scores = jnp.einsum('gsd,kd->gsk', query_group, key_group) * scale
        scores = jnp.where(allowed[None], scores, -1e+30)
        largest = lax.optimization_barrier(jnp.max(scores, axis=-1, keepdims=True))
        weights = jnp.exp(scores - largest)
        total = lax.optimization_barrier(jnp.sum(weights, axis=-1, keepdims=True))
        probs = lax.optimization_barrier(weights.astype(jnp.bfloat16)).astype(jnp.float32)
        mixed = jnp.einsum('gsk,kd->gsd', probs, value_group)
        return (mixed / total).astype(jnp.bfloat16)
    heads = lax.map(one_head, (grouped, key_heads, value_heads))
    return heads.transpose(2, 0, 1, 3).reshape(count, QH * HD)

def reference(prompt_k, prompt_v, prompt_mask, shared_kv, shared_len, send_pick, unique_q, unique_kv, unique_owner):
    owner_of = unique_owner[:, 0].astype(jnp.int32)
    positions = jnp.arange(ROWS, dtype=jnp.int32)
    source = positions // UNQ_DEV
    grid_owner = owner_of.reshape(N_BRANCH, UNQ_DEV)
    in_device = jnp.arange(UNQ_DEV, dtype=jnp.int32)
    earlier = (grid_owner[:, :, None] == grid_owner[:, None, :]) & (in_device[None, None, :] < in_device[None, :, None])
    rank = lax.optimization_barrier(jnp.sum(earlier.astype(jnp.int32), axis=2)).reshape(ROWS).astype(jnp.int32)
    slot_index = (source * CAP + rank).astype(jnp.int32)
    width = N_BRANCH * CAP
    query_slots = jnp.zeros((N_BRANCH, width, QW), jnp.bfloat16).at[owner_of, slot_index].set(unique_q)
    pair_slots = jnp.zeros((N_BRANCH, width, 2 * KVW), jnp.bfloat16).at[owner_of, slot_index].set(unique_kv)
    live_slots = jnp.zeros((N_BRANCH, width), jnp.int32).at[owner_of, slot_index].set(1)
    by_owner = shared_kv.reshape(N_BRANCH, RES_DEV, RLEN, 2 * KVW)
    len_by_owner = shared_len.reshape(N_BRANCH, RES_DEV)
    owners = jnp.arange(N_BRANCH, dtype=jnp.int32)
    within = jnp.arange(RLEN, dtype=jnp.int32)
    slot_range = jnp.arange(width, dtype=jnp.int32)
    causal = slot_range[None, :] <= slot_range[:, None]

    def one_branch(branch_id):
        picked = send_pick[:, branch_id]
        safe = jnp.maximum(picked, 0).astype(jnp.int32)
        fetched = by_owner[owners, safe].reshape(N_BRANCH * RLEN, 2 * KVW)
        live_len = jnp.where(picked >= 0, len_by_owner[owners, safe], 0)
        shared_ok = (within[None, :] < live_len[:, None]).reshape(N_BRANCH * RLEN)
        block_ok = jnp.repeat(prompt_mask[branch_id] > 0, PB)
        unique_ok = causal & (live_slots[branch_id] > 0)[None, :]
        allowed = jnp.concatenate([jnp.broadcast_to(block_ok[None], (width, PLEN)), jnp.broadcast_to(shared_ok[None], (width, N_BRANCH * RLEN)), unique_ok], axis=1)
        pairs = pair_slots[branch_id]
        key_rows = jnp.concatenate([prompt_k[branch_id], fetched[:, :KVW], pairs[:, :KVW]], axis=0)
        value_rows = jnp.concatenate([prompt_v[branch_id], fetched[:, KVW:], pairs[:, KVW:]], axis=0)
        return attend(query_slots[branch_id], key_rows, value_rows, allowed)
    results = lax.map(one_branch, owners)
    return results[owner_of, slot_index]
```

```python
import functools
import math

import jax
import jax.numpy as jnp
from jax import lax
from jax.experimental import pallas as pl
from jax.experimental.pallas import tpu as pltpu
from jax.sharding import PartitionSpec as P

HD = 128
GRP = 8
NEG = -1e30
MESH = pl.DeviceIdType.MESH


def kernel(
    n, across, cap, rlen, res, heads,
    owner_ref, pick_ref, len_ref, mask_ref, q_hbm, kv_hbm, shared_hbm, pk_hbm, pv_hbm,
    out_hbm,
    q_ref, kv_ref, pk, pv, flat, by_row, slot_of, pbias, meta_ref, xs, xr, mr, gath, tail, kslot,
    acc, stat, ox, out_ref,
    lsem, osem, xsend, xrecv, msend, mrecv, gsend, grecv, srecv, rsend, rrecv, *orx,
):
    me = lax.axis_index("branch")
    kvh = heads // GRP
    pairs = kvh // 2
    width = n * cap
    rows = width * GRP
    kvw = kvh * HD
    line = n // (2 * across)
    core = lax.rem(me, 2)
    chip = me // 2
    y = lax.rem(chip, across)
    z = chip // across
    sibling = me + 1 - 2 * core
    tail_n = tail.shape[0]
    scale = math.log2(math.e) / math.sqrt(HD)
    two = 2 * GRP
    barrier = pltpu.get_barrier_semaphore()

    def greet(i, c):
        pl.semaphore_signal(
            barrier, inc=1, device_id={"branch": lax.rem(me + i, n)}, device_id_type=MESH
        )
        return c

    lax.fori_loop(1, n, greet, 0)

    copy_s = pltpu.make_async_copy(shared_hbm, gath.at[me], lsem.at[0])
    copy_q = pltpu.make_async_copy(q_hbm, q_ref, lsem.at[1])
    copy_u = pltpu.make_async_copy(kv_hbm, kv_ref, lsem.at[2])
    copy_k = pltpu.make_async_copy(pk_hbm.at[0], pk, lsem.at[3])
    copy_v = pltpu.make_async_copy(pv_hbm.at[0], pv, lsem.at[4])
    copy_s.start()
    copy_q.start()
    copy_u.start()
    copy_k.start()
    copy_v.start()

    def ship(source, e, target, recv):
        return pltpu.make_async_remote_copy(
            src_ref=gath.at[source, e], dst_ref=gath.at[source, e],
            send_sem=gsend.at[0], recv_sem=recv,
            device_id={"branch": target}, device_id_type=MESH,
        )

    def slot(source, e):
        return grecv.at[(source // 2) * res + e]

    def member(zz, yy, cc):
        return (zz * across + yy) * 2 + cc

    def spread(zs, e, act):
        source = member(zs, y, core)
        recv = slot(source, e)

        @pl.when(jnp.logical_and(zs <= z, z + 1 < line))
        def _():
            act(ship(source, e, member(lax.rem(z + 1, line), y, core), recv))

        @pl.when(jnp.logical_and(zs >= z, z >= 1))
        def _():
            act(ship(source, e, member(lax.rem(z + line - 1, line), y, core), recv))

        for d in range(1, across):
            act(ship(source, e, member(z, lax.rem(y + d, across), core), recv))
        act(ship(source, e, sibling, srecv.at[0]))

    def arrived(source, e):
        ship(source, e, sibling, slot(source, e)).wait_recv()

    begin = lambda copy: copy.start()
    finish = lambda copy: copy.wait_send()

    def on_line(t, act, waits):
        for e in range(res):
            for up in (0, 1):
                zs = z - t if up == 0 else z + t
                ok = zs >= 0 if up == 0 else zs < line

                @pl.when(ok)
                def _():
                    zc = lax.rem(zs + line, line)
                    if waits:
                        arrived(member(zc, y, core), e)
                    spread(zc, e, act)

    def cross(zs, act, waits):
        for d in range(1, across):
            source = member(zs, lax.rem(y + d, across), core)
            for e in range(res):
                if waits:
                    arrived(source, e)
                act(ship(source, e, sibling, srecv.at[0]))

    def off_line(t, act, waits):
        @pl.when(z - t >= 0)
        def _():
            cross(lax.rem(z - t + line, line), act, waits)

        @pl.when(jnp.logical_and(z + t < line, t > 0))
        def _():
            cross(lax.rem(z + t, line), act, waits)

    cuts = [1 + (line - 1) * j // 3 for j in range(4)]

    def on_lines(j):
        def one(t, c):
            on_line(t, begin, True)
            return c

        lax.fori_loop(cuts[j], cuts[j + 1], one, 0)

    def off_lines(j):
        def one(t, c):
            off_line(t, begin, True)
            return c

        if across > 1:
            lax.fori_loop(cuts[j] if j >= 0 else 0, cuts[j + 1], one, 0)

    def group(g):
        lo = 0 if g == 0 else g * two + 2 * kvh
        return slice(lo, (g + 1) * two + 2 * kvh)

    def x_copy(g, b, at):
        return pltpu.make_async_remote_copy(
            src_ref=xs.at[pl.ds(b * cap, cap), group(g)],
            dst_ref=xr.at[pl.ds(at * cap, cap), group(g)],
            send_sem=xsend.at[0], recv_sem=xrecv.at[g],
            device_id={"branch": b}, device_id_type=MESH,
        )

    def m_copy(b, at):
        return pltpu.make_async_remote_copy(
            src_ref=meta_ref.at[b], dst_ref=mr.at[at],
            send_sem=msend.at[0], recv_sem=mrecv.at[0],
            device_id={"branch": b}, device_id_type=MESH,
        )

    def send_x(g):
        def one(i, c):
            b = lax.rem(me + i, n)
            x_copy(g, b, me).start()
            if g == 0:
                m_copy(b, me).start()
            return c

        lax.fori_loop(1, n, one, 0)

    others = pl.ds(0, (n - 1) * cap)

    def x_all(g):
        return pltpu.make_async_remote_copy(
            src_ref=xs.at[others, group(g)], dst_ref=xr.at[others, group(g)],
            send_sem=xsend.at[0], recv_sem=xrecv.at[g],
            device_id={"branch": sibling}, device_id_type=MESH,
        )

    def m_all():
        return pltpu.make_async_remote_copy(
            src_ref=meta_ref.at[pl.ds(0, n - 1)], dst_ref=mr.at[pl.ds(0, n - 1)],
            send_sem=msend.at[0], recv_sem=mrecv.at[0],
            device_id={"branch": sibling}, device_id_type=MESH,
        )

    def sib_all():
        half = gath.at[pl.ds(0, n // 2)]
        return pltpu.make_async_remote_copy(
            src_ref=half, dst_ref=half, send_sem=gsend.at[0], recv_sem=srecv.at[0],
            device_id={"branch": sibling}, device_id_type=MESH,
        )

    copy_s.wait()
    pl.semaphore_wait(barrier, n - 1)
    for e in range(res):
        spread(z, e, begin)

    count = q_ref.shape[0]
    per = heads + 2 * kvh
    some = min(count, 16)

    def number(j, c):
        mine = owner_ref[j]
        rank = lax.fori_loop(
            0, j, lambda i, r: r + jnp.where(owner_ref[i] == mine, 1, 0), jnp.int32(0)
        )
        slot_of[j] = mine * cap + rank
        return c

    lax.fori_loop(0, count, number, 0)
    copy_q.wait()
    copy_u.wait()

    for r in range(0, count, some):
        for h in range(per):
            ref, g = (q_ref, h) if h < heads else (kv_ref, h - heads)
            at = h if h < two else h + 2 * kvh if h < heads else two + g
            flat[pl.ds(at, some, stride=per), :] = ref[
                r : r + some, g * HD : (g + 1) * HD
            ].astype(jnp.float32)
        for i in range(some):
            by_row[r + i] = flat[i * per : (i + 1) * per].astype(jnp.bfloat16)

    lane = lax.broadcasted_iota(jnp.int32, (1, HD), 1)

    def place(b, c):
        def scan(r, found):
            for u in range(some):
                i = r * some + u
                hit = owner_ref[i] == b
                rows_at, seen = found[:cap], found[cap]
                rows_at = [
                    jnp.where(jnp.logical_and(hit, seen == k), i, at)
                    for k, at in enumerate(rows_at)
                ]
                found = (*rows_at, seen + jnp.where(hit, 1, 0))
            return found

        found = lax.fori_loop(0, count // some, scan, (jnp.int32(0),) * (cap + 1))
        pick = pick_ref[0, b]
        length = jnp.int32(0)
        for e in range(res):
            length = jnp.where(pick == e, len_ref[e], length)
        meta_ref[b] = jnp.where(
            lane == 0, pick, jnp.where(lane == 1, length, jnp.where(found[cap] > lane - 2, 1, 0))
        )
        for k in range(cap):
            xs[b * cap + k] = by_row[found[k]]
        return c

    lax.fori_loop(0, n, place, 0)
    blocks = mask_ref.shape[1]
    block = pk.shape[0] // blocks
    for g in range(blocks):
        pbias[:, g * block : (g + 1) * block] = jnp.full(
            (1, block), jnp.where(mask_ref[0, g] > 0, 0.0, NEG), jnp.float32
        )

    def part(ref, b):
        return ref.at[pl.ds(b * cap, cap)]

    own_x = pltpu.make_async_copy(part(xs, me), part(xr, me), lsem.at[5])
    own_m = pltpu.make_async_copy(meta_ref.at[me], mr.at[me], lsem.at[6])

    def queries(p):
        lo = 0 if p == 0 else p * two + 2 * kvh
        both = xr[:, lo : lo + two, :].astype(jnp.float32)
        return [
            both[:, k * GRP : (k + 1) * GRP].reshape(rows, HD).astype(jnp.bfloat16)
            for k in range(2)
        ]

    def scores(q, k):
        return lax.dot_general(q, k, (((1,), (1,)), ((), ())), preferred_element_type=jnp.float32)

    half = lax.broadcasted_iota(jnp.int32, (rows, HD), 1) < HD // 2

    def prompt_pair(p):
        for k, q in enumerate(queries(p)):
            h = 2 * p + k
            cols = slice(h * HD, (h + 1) * HD)
            s = scores(q, pk[:, cols]) * scale + pbias[...]
            m = jnp.max(s, axis=-1, keepdims=True)
            w = jnp.exp2(s - m)
            stat[h] = jnp.where(half, m, jnp.sum(w, axis=-1, keepdims=True))
            acc[h] = jnp.dot(
                w.astype(jnp.bfloat16), pv[:, cols], preferred_element_type=jnp.float32
            )

    def tail_keys():
        kv_at = slice(two, two + 2 * kvh)
        flat[: width * 2 * kvh] = (
            xr[:, kv_at, :].astype(jnp.float32).reshape(width * 2 * kvh, HD)
        )
        for j in range(2 * kvh):
            tail[n * rlen : n * rlen + width, j * HD : (j + 1) * HD] = flat[
                pl.ds(j, width, stride=2 * kvh), :
            ].astype(jnp.bfloat16)
        col = lax.broadcasted_iota(jnp.int32, (1, tail_n), 1)

        def limits(s, carry):
            length, live = carry
            meta = mr[s]
            length = jnp.where(col // rlen == s, meta[:, 1:2], length)
            for k in range(cap):
                live = jnp.where(col == n * rlen + s * cap + k, meta[:, 2 + k : 3 + k], live)
            return length, live

        zero = jnp.zeros((1, tail_n), jnp.int32)
        length, live = lax.fori_loop(0, n, limits, (zero, zero))
        shared_ok = jnp.logical_and(col < n * rlen, lax.rem(col, rlen) < length)
        kslot[...] = jnp.where(shared_ok, -1, jnp.where(live > 0, col - n * rlen, width))

    row_slot = lax.broadcasted_iota(jnp.int32, (rows, 1), 0) // GRP

    def choose(t, c):
        two_of = []
        for s in (2 * t, 2 * t + 1):
            pick = mr[s][:, 0:1]
            chosen = gath[s, 0].astype(jnp.float32)
            for e in range(1, res):
                chosen = jnp.where(pick == e, gath[s, e].astype(jnp.float32), chosen)
            two_of.append(chosen)
        tail[pl.ds(pl.multiple_of(t * 2 * rlen, 16), 2 * rlen), :] = jnp.concatenate(
            two_of, axis=0
        ).astype(jnp.bfloat16)
        return c

    def tail_pair(p):
        done = []
        for k, q in enumerate(queries(p)):
            h = 2 * p + k
            keys = tail[:, h * HD : (h + 1) * HD]
            values = tail[:, kvw + h * HD : kvw + (h + 1) * HD]
            s = jnp.where(kslot[...] <= row_slot, scores(q, keys) * scale, NEG)
            before = stat[h][:, :1]
            m = jnp.maximum(before, jnp.max(s, axis=-1, keepdims=True))
            w = jnp.exp2(s - m)
            keep = jnp.exp2(before - m)
            total = stat[h][:, HD // 2 : HD // 2 + 1] * keep + jnp.sum(w, axis=-1, keepdims=True)
            mixed = acc[h] * keep + jnp.dot(
                w.astype(jnp.bfloat16), values, preferred_element_type=jnp.float32
            )
            done.append((mixed / total).reshape(width, GRP, HD))
        ox[:, p * two : (p + 1) * two, :] = jnp.concatenate(done, axis=1).astype(jnp.bfloat16)

    def r_copy(p, b, at):
        cut = slice(p * two, (p + 1) * two)
        return pltpu.make_async_remote_copy(
            src_ref=ox.at[pl.ds(b * cap, cap), cut], dst_ref=orx[p].at[pl.ds(at * cap, cap)],
            send_sem=rsend.at[0], recv_sem=rrecv.at[p],
            device_id={"branch": b}, device_id_type=MESH,
        )

    def r_all(p):
        cut = slice(p * two, (p + 1) * two)
        return pltpu.make_async_remote_copy(
            src_ref=ox.at[others, cut], dst_ref=orx[p].at[others],
            send_sem=rsend.at[0], recv_sem=rrecv.at[p],
            device_id={"branch": sibling}, device_id_type=MESH,
        )

    def own_r(p):
        cut = slice(p * two, (p + 1) * two)
        return pltpu.make_async_copy(
            ox.at[pl.ds(me * cap, cap), cut], orx[p].at[pl.ds(me * cap, cap)], osem.at[p]
        )

    def give_back(p):
        def one(i, c):
            r_copy(p, lax.rem(me + i, n), me).start()
            return c

        lax.fori_loop(1, n, one, 0)
        own_r(p).start()

    def prompt(p):
        x_all(p).wait_recv()
        if p == 0:
            m_all().wait_recv()
            own_x.wait()
            own_m.wait()
            copy_k.wait()
            copy_v.wait()
        prompt_pair(p)

    def put(p):
        cols = slice(p * two * HD, (p + 1) * two * HD)
        return pltpu.make_async_copy(
            out_ref.at[:, cols], out_hbm.at[:, cols], osem.at[pairs + p]
        )

    own_x.start()
    own_m.start()
    on_lines(0)
    send_x(0)
    tail[...] = jnp.zeros_like(tail)
    off_lines(-1)
    on_lines(1)
    send_x(1)
    for g in range(2, pairs - 1):
        send_x(g)
    off_lines(0)
    on_lines(2)
    send_x(pairs - 1)
    prompt(0)
    tail_keys()
    off_lines(1)
    for p in range(1, pairs - 1):
        prompt(p)
    off_lines(2)
    sib_all().wait_recv()
    lax.fori_loop(0, n // 2, choose, 0)
    for p in range(pairs):
        if p == pairs - 1:
            prompt(p)
        tail_pair(p)
        give_back(p)

    for g in range(pairs):
        x_all(g).wait_send()
    m_all().wait_send()
    for e in range(res):
        spread(z, e, finish)

    def relayed(t, c):
        on_line(t, finish, False)
        return c

    lax.fori_loop(1, line, relayed, 0)

    def crossed(t, c):
        off_line(t, finish, False)
        return c

    if across > 1:
        lax.fori_loop(0, line, crossed, 0)

    for p in range(pairs):
        r_all(p).wait_recv()
        own_r(p).wait()
        for r in range(0, count, some):
            for i in range(some):
                flat[i * two : (i + 1) * two] = orx[p][slot_of[r + i]].astype(jnp.float32)
            for h in range(two):
                at = (p * two + h) * HD
                out_ref[r : r + some, at : at + HD] = flat[
                    pl.ds(h, some, stride=two), :
                ].astype(jnp.bfloat16)
        put(p).start()
    for p in range(pairs):
        r_all(p).wait_send()
    for p in range(pairs):
        put(p).wait()


def body(
    across, prompt_k, prompt_v, prompt_mask, shared_kv, shared_len, send_pick,
    unique_q, unique_kv, unique_owner,
):
    n = lax.axis_size("branch")
    rows = unique_q.shape[0]
    cap = 2 * rows // n
    width = n * cap
    res, rlen = shared_kv.shape[:2]
    heads = unique_q.shape[1] // HD
    kvh = unique_kv.shape[1] // (2 * HD)
    pairs = kvh // 2
    plen = prompt_k.shape[1]
    tail_n = -(-(n * rlen + width) // 128) * 128
    qrows = width * GRP
    smem = pl.BlockSpec(memory_space=pltpu.SMEM)
    anyp = pl.BlockSpec(memory_space=pl.ANY)
    bf, f32 = jnp.bfloat16, jnp.float32
    dma = pltpu.SemaphoreType.DMA
    out = pl.pallas_call(
        functools.partial(kernel, n, across, cap, rlen, res, heads),
        out_shape=jax.ShapeDtypeStruct((rows, heads * HD), bf),
        in_specs=[smem, smem, smem, smem, anyp, anyp, anyp, anyp, anyp],
        out_specs=anyp,
        scratch_shapes=[
            pltpu.VMEM(unique_q.shape, bf),
            pltpu.VMEM(unique_kv.shape, bf),
            pltpu.VMEM(prompt_k.shape[1:], bf),
            pltpu.VMEM(prompt_v.shape[1:], bf),
            pltpu.VMEM((max(min(rows, 16) * (heads + 2 * kvh), width * 2 * kvh), HD), f32),
            pltpu.VMEM((rows, heads + 2 * kvh, HD), bf),
            pltpu.SMEM((rows,), jnp.int32),
            pltpu.VMEM((1, plen), f32),
            pltpu.VMEM((n, 1, HD), jnp.int32),
            pltpu.VMEM((width, heads + 2 * kvh, HD), bf),
            pltpu.VMEM((width, heads + 2 * kvh, HD), bf),
            pltpu.VMEM((n, 1, HD), jnp.int32),
            pltpu.VMEM((n,) + shared_kv.shape, bf),
            pltpu.VMEM((tail_n, 2 * kvh * HD), bf),
            pltpu.VMEM((1, tail_n), jnp.int32),
            pltpu.VMEM((kvh, qrows, HD), f32),
            pltpu.VMEM((kvh, qrows, HD), f32),
            pltpu.VMEM((width, heads, HD), bf),
            pltpu.VMEM((rows, heads * HD), bf),
            dma((7,)),
            dma((2 * pairs,)),
            dma((1,)),
            dma((pairs,)),
            dma((1,)),
            dma((1,)),
            dma((1,)),
            dma((n // 2 * res,)),
            dma((1,)),
            dma((1,)),
            dma((pairs,)),
            *[pltpu.VMEM((width, 2 * GRP, HD), bf)] * pairs,
        ],
        compiler_params=pltpu.CompilerParams(
            collective_id=0, has_side_effects=True, vmem_limit_bytes=67043328
        ),
    )(
        unique_owner.reshape(rows), send_pick, shared_len, prompt_mask,
        unique_q, unique_kv, shared_kv, prompt_k, prompt_v,
    )
    return out


def chips_across(mesh):
    devices = mesh.devices.reshape(-1, mesh.shape["branch"])[0]
    try:
        places = [tuple(d.coords) for d in devices[::2]]
    except (AttributeError, TypeError):
        return 1
    return sum(1 for p in places if p[2] == places[0][2])


def solution(mesh):
    spec1, spec2, spec3 = (P(("groups", "branch"), *(None,) * k) for k in range(3))
    in_specs = (spec3, spec3, spec2, spec3, spec1, spec2, spec2, spec2, spec2)
    return jax.shard_map(
        functools.partial(body, chips_across(mesh)),
        mesh=mesh, in_specs=in_specs, out_specs=spec2, check_vma=False,
    )
```

```python
import functools
import math

import jax
import jax.numpy as jnp
from jax import lax
from jax.experimental import pallas as pl
from jax.experimental.pallas import tpu as pltpu
from jax.sharding import PartitionSpec as P

HD = 128
GRP = 8
NEG = -1e30
MESH = pl.DeviceIdType.MESH


def kernel(
    n, across, cap, rlen, res, heads,
    owner_hbm, pick_hbm, len_hbm, mask_hbm, q_hbm, kv_hbm, shared_hbm, pk_hbm, pv_hbm,
    out_ref,
    owner_ref, pick_ref, len_ref, mask_ref, meta_in,
    q_ref, kv_ref, pk, pv, flat, by_row, slot_of, pbias, tbias, meta_ref, xs, xr, mr, tail, kslot,
    ox, lsem, osem, xsend, xrecv, msend, mrecv, gsend, grecv, srecv, rsend, rrecv, *by_group,
):
    me = lax.axis_index("branch")
    kvh = heads // GRP
    pairs = kvh // 2
    orx, gath = by_group[:pairs], by_group[pairs:]
    width = n * cap
    rows = width * GRP
    kvw = kvh * HD
    line = n // (2 * across)
    core = lax.rem(me, 2)
    chip = me // 2
    y = lax.rem(chip, across)
    z = chip // across
    sibling = me + 1 - 2 * core
    tail_n = tail.shape[1]
    scale = math.log2(math.e) / math.sqrt(HD)
    two = 2 * GRP
    barrier = pltpu.get_barrier_semaphore()

    def greet(i, c):
        pl.semaphore_signal(
            barrier, inc=1, device_id={"branch": lax.rem(me + i, n)}, device_id_type=MESH
        )
        return c

    lax.fori_loop(1, n, greet, 0)

    gw = 2 * HD

    def load_shared(g, part):
        return pltpu.make_async_copy(
            shared_hbm.at[:, :, pl.ds(part * kvw + g * gw, gw)],
            gath[g].at[me, :, :, pl.ds(part * gw, gw)],
            lsem.at[9 + g],
        )

    copy_q = pltpu.make_async_copy(q_hbm, q_ref, lsem.at[4])
    copy_u = pltpu.make_async_copy(kv_hbm, kv_ref, lsem.at[5])
    copy_k = pltpu.make_async_copy(pk_hbm.at[0], pk, lsem.at[6])
    copy_v = pltpu.make_async_copy(pv_hbm.at[0], pv, lsem.at[7])
    for g in range(pairs):
        for part in range(2):
            load_shared(g, part).start()
    small = [
        pltpu.make_async_copy(src, dst, lsem.at[i])
        for i, (src, dst) in enumerate(
            [(owner_hbm, owner_ref), (pick_hbm, pick_ref), (len_hbm, len_ref), (mask_hbm, mask_ref)]
        )
    ]
    for copy in small:
        copy.start()
    copy_q.start()
    copy_u.start()
    copy_k.start()
    copy_v.start()

    def ship(source, g, target, recv):
        return pltpu.make_async_remote_copy(
            src_ref=gath[g].at[source], dst_ref=gath[g].at[source],
            send_sem=gsend.at[0], recv_sem=recv,
            device_id={"branch": target}, device_id_type=MESH,
        )

    def slot(source, g):
        return grecv.at[(source // 2) * pairs + g]

    def member(zz, yy, cc):
        return (zz * across + yy) * 2 + cc

    def spread(zs, g, act):
        source = member(zs, y, core)
        recv = slot(source, g)

        @pl.when(jnp.logical_and(zs <= z, z + 1 < line))
        def _():
            act(ship(source, g, member(lax.rem(z + 1, line), y, core), recv))

        @pl.when(jnp.logical_and(zs >= z, z >= 1))
        def _():
            act(ship(source, g, member(lax.rem(z + line - 1, line), y, core), recv))

        for d in range(1, across):
            act(ship(source, g, member(z, lax.rem(y + d, across), core), recv))
        act(ship(source, g, sibling, srecv.at[g]))

    def arrived(source, g):
        ship(source, g, sibling, slot(source, g)).wait_recv()

    begin = lambda copy: copy.start()
    finish = lambda copy: copy.wait_send()

    def on_line(t, g, act, waits):
        for up in (0, 1):
            zs = z - t if up == 0 else z + t
            ok = zs >= 0 if up == 0 else zs < line

            @pl.when(ok)
            def _():
                zc = lax.rem(zs + line, line)
                if waits:
                    arrived(member(zc, y, core), g)
                spread(zc, g, act)

    def cross(zs, g, act, waits):
        for d in range(1, across):
            source = member(zs, lax.rem(y + d, across), core)
            if waits:
                arrived(source, g)
            act(ship(source, g, sibling, srecv.at[g]))

    def off_line(t, g, act, waits):
        @pl.when(z - t >= 0)
        def _():
            cross(lax.rem(z - t + line, line), g, act, waits)

        @pl.when(jnp.logical_and(z + t < line, t > 0))
        def _():
            cross(lax.rem(z + t, line), g, act, waits)

    cuts = [0] + [1 + (line - 1) * j // 3 for j in range(4)]

    def own(g):
        spread(z, g, begin)

    def on_lines(g, j):
        def one(t, c):
            on_line(t, g, begin, True)
            return c

        lax.fori_loop(cuts[j], cuts[j + 1], one, 0)

    def off_lines(g, j):
        def one(t, c):
            off_line(t, g, begin, True)
            return c

        if across > 1:
            lax.fori_loop(cuts[j], cuts[j + 1], one, 0)

    def group(g):
        lo = 0 if g == 0 else g * two + 2 * kvh
        return slice(lo, (g + 1) * two + 2 * kvh)

    def x_copy(g, b, at):
        return pltpu.make_async_remote_copy(
            src_ref=xs.at[pl.ds(b * cap, cap), group(g)],
            dst_ref=xr.at[pl.ds(at * cap, cap), group(g)],
            send_sem=xsend.at[0], recv_sem=xrecv.at[g],
            device_id={"branch": b}, device_id_type=MESH,
        )

    def m_copy(b, at):
        return pltpu.make_async_remote_copy(
            src_ref=meta_ref.at[b], dst_ref=mr.at[at],
            send_sem=msend.at[0], recv_sem=mrecv.at[0],
            device_id={"branch": b}, device_id_type=MESH,
        )

    def send_to(g, b):
        x_copy(g, b, me).start()
        if g == 0:
            m_copy(b, me).start()

    def send_x(g, d):
        def one(i, c):
            at = lax.rem(2 * z + core + i, 2 * line)
            send_to(g, member(at // 2, lax.rem(y + d, across), lax.rem(at, 2)))
            return c

        lax.fori_loop(0 if d else 1, 2 * line, one, 0)

    def send_near(g):
        send_x(g, 0)

    def send_far(g):
        for d in range(1, across):
            send_x(g, d)

    others = pl.ds(0, (n - 1) * cap)

    def x_all(g):
        return pltpu.make_async_remote_copy(
            src_ref=xs.at[others, group(g)], dst_ref=xr.at[others, group(g)],
            send_sem=xsend.at[0], recv_sem=xrecv.at[g],
            device_id={"branch": sibling}, device_id_type=MESH,
        )

    def m_all():
        return pltpu.make_async_remote_copy(
            src_ref=meta_ref.at[pl.ds(0, n - 1)], dst_ref=mr.at[pl.ds(0, n - 1)],
            send_sem=msend.at[0], recv_sem=mrecv.at[0],
            device_id={"branch": sibling}, device_id_type=MESH,
        )

    def sib_all(g):
        half = gath[g].at[pl.ds(0, n // 2)]
        return pltpu.make_async_remote_copy(
            src_ref=half, dst_ref=half, send_sem=gsend.at[0], recv_sem=srecv.at[g],
            device_id={"branch": sibling}, device_id_type=MESH,
        )

    def loaded(g):
        mine = gath[g].at[me]
        pltpu.make_async_copy(mine, mine, lsem.at[9 + g]).wait()

    loaded(0)
    pl.semaphore_wait(barrier, n - 1)
    own(0)
    for g in range(1, pairs):
        loaded(g)
        own(g)
    for copy in small:
        copy.wait()
    count = q_ref.shape[0]
    per = heads + 2 * kvh
    some = min(count, 16)

    def number(j, c):
        mine = owner_ref[j]
        rank = lax.fori_loop(
            0, j, lambda i, r: r + jnp.where(owner_ref[i] == mine, 1, 0), jnp.int32(0)
        )
        slot_of[j] = mine * cap + rank
        return c

    lax.fori_loop(0, count, number, 0)
    copy_q.wait()
    copy_u.wait()

    for r in range(0, count, some):
        for h in range(per):
            ref, g = (q_ref, h) if h < heads else (kv_ref, h - heads)
            at = h if h < two else h + 2 * kvh if h < heads else two + g
            flat[pl.ds(at, some, stride=per), :] = ref[
                r : r + some, g * HD : (g + 1) * HD
            ].astype(jnp.float32)
        for i in range(some):
            by_row[r + i] = flat[i * per : (i + 1) * per].astype(jnp.bfloat16)

    lane = lax.broadcasted_iota(jnp.int32, (1, HD), 1)

    def place(b, c):
        def scan(r, found):
            for u in range(some):
                i = r * some + u
                hit = owner_ref[i] == b
                rows_at, seen = found[:cap], found[cap]
                rows_at = [
                    jnp.where(jnp.logical_and(hit, seen == k), i, at)
                    for k, at in enumerate(rows_at)
                ]
                found = (*rows_at, seen + jnp.where(hit, 1, 0))
            return found

        found = lax.fori_loop(0, count // some, scan, (jnp.int32(0),) * (cap + 1))
        pick = pick_ref[0, b]
        length = jnp.int32(0)
        for e in range(res):
            length = jnp.where(pick == e, len_ref[e], length)
        meta_ref[b] = jnp.where(
            lane == 0, pick, jnp.where(lane == 1, length, jnp.where(found[cap] > lane - 2, 1, 0))
        )
        for k in range(cap):
            xs[b * cap + k] = by_row[found[k]]
        return c

    lax.fori_loop(0, n, place, 0)
    blocks = mask_ref.shape[1]
    block = pk.shape[0] // blocks
    for g in range(blocks):
        pbias[:, g * block : (g + 1) * block] = jnp.full(
            (1, block), jnp.where(mask_ref[0, g] > 0, 0.0, NEG), jnp.float32
        )

    def part(ref, b):
        return ref.at[pl.ds(b * cap, cap)]

    own_x = pltpu.make_async_copy(part(xs, me), part(xr, me), osem.at[pairs])
    own_m = pltpu.make_async_copy(meta_ref.at[me], mr.at[me], osem.at[pairs + 1])

    def queries(p):
        lo = 0 if p == 0 else p * two + 2 * kvh
        both = xr[:, lo : lo + two, :].astype(jnp.float32)
        return [
            both[:, k * GRP : (k + 1) * GRP].reshape(rows, HD).astype(jnp.bfloat16)
            for k in range(2)
        ]

    def scores(q, k):
        return lax.dot_general(q, k, (((1,), (1,)), ((), ())), preferred_element_type=jnp.float32)

    copy_m = pltpu.make_async_copy(mr, meta_in, osem.at[pairs + 2])

    def metas():
        m_all().wait_recv()
        own_m.wait()
        copy_m.start()

    def tail_keys():
        copy_m.wait()
        col = lax.broadcasted_iota(jnp.int32, (1, tail_n), 1)
        owner, at_row = col // rlen, lax.rem(col, rlen)
        some_s = min(n, 16)

        def limits(i, carry):
            length, live = carry
            for u in range(some_s):
                s = i * some_s + u
                length = jnp.where(owner == s, meta_in[s, 0, 1], length)
                for k in range(cap):
                    live = jnp.where(
                        col == n * rlen + s * cap + k, meta_in[s, 0, 2 + k], live
                    )
            return length, live

        zero = jnp.zeros((1, tail_n), jnp.int32)
        length, live = lax.fori_loop(0, n // some_s, limits, (zero, zero))
        shared_ok = jnp.logical_and(col < n * rlen, at_row < length)
        tbias[...] = jnp.where(shared_ok, 0.0, NEG)
        kslot[...] = jnp.where(shared_ok, -1, jnp.where(live > 0, col - n * rlen, width))
        x_all(0).wait_recv()
        own_x.wait()
        kv_at = slice(two, two + 2 * kvh)
        flat[: width * 2 * kvh] = (
            xr[:, kv_at, :].astype(jnp.float32).reshape(width * 2 * kvh, HD)
        )
        for j in range(2 * kvh):
            at = j % 2 + 2 * (j // kvh)
            tail[j % kvh // 2, n * rlen : n * rlen + width, at * HD : (at + 1) * HD] = flat[
                pl.ds(j, width, stride=2 * kvh), :
            ].astype(jnp.bfloat16)

    row_slot = lax.broadcasted_iota(jnp.int32, (rows, 1), 0) // GRP
    fixed = n * rlen // HD * HD

    def choose(g):
        sib_all(g).wait_recv()
        block = min(n, 16)

        def one(i, c):
            for t in range(0, block, 2):
                two_of = [
                    gath[g][s, jnp.maximum(meta_in[s, 0, 0], 0)].astype(jnp.float32)
                    for s in (i * block + t, i * block + t + 1)
                ]
                at = pl.multiple_of(i * block * rlen + t * rlen, 16)
                tail[g, pl.ds(at, 2 * rlen), :] = jnp.concatenate(two_of, axis=0).astype(
                    jnp.bfloat16
                )
            return c

        lax.fori_loop(0, n // block, one, 0)

    def attend(p):
        if p == 0:
            copy_k.wait()
            copy_v.wait()
        else:
            x_all(p).wait_recv()
        done = []
        for k, q in enumerate(queries(p)):
            h = 2 * p + k
            cols = slice(h * HD, (h + 1) * HD)
            keys = tail[p, :, k * HD : (k + 1) * HD]
            values = tail[p, :, (2 + k) * HD : (3 + k) * HD]
            sp = scores(q, pk[:, cols]) * scale + pbias[...]
            st = scores(q, keys) * scale
            sf = st[:, :fixed] + tbias[:, :fixed]
            su = jnp.where(kslot[:, fixed:] <= row_slot, st[:, fixed:], NEG)
            m = jnp.maximum(
                jnp.max(sp, axis=-1, keepdims=True),
                jnp.maximum(
                    jnp.max(sf, axis=-1, keepdims=True), jnp.max(su, axis=-1, keepdims=True)
                ),
            )
            wp = jnp.exp2(sp - m)
            wt = jnp.exp2(jnp.concatenate([sf, su], axis=1) - m)
            total = jnp.sum(wp, axis=-1, keepdims=True) + jnp.sum(wt, axis=-1, keepdims=True)
            mixed = jnp.dot(
                wp.astype(jnp.bfloat16), pv[:, cols], preferred_element_type=jnp.float32
            ) + jnp.dot(wt.astype(jnp.bfloat16), values, preferred_element_type=jnp.float32)
            done.append((mixed / total).reshape(width, GRP, HD))
        ox[:, p * two : (p + 1) * two, :] = jnp.concatenate(done, axis=1).astype(jnp.bfloat16)

    def r_copy(p, b, at):
        cut = slice(p * two, (p + 1) * two)
        return pltpu.make_async_remote_copy(
            src_ref=ox.at[pl.ds(b * cap, cap), cut], dst_ref=orx[p].at[pl.ds(at * cap, cap)],
            send_sem=rsend.at[0], recv_sem=rrecv.at[p],
            device_id={"branch": b}, device_id_type=MESH,
        )

    def r_all(p):
        cut = slice(p * two, (p + 1) * two)
        return pltpu.make_async_remote_copy(
            src_ref=ox.at[others, cut], dst_ref=orx[p].at[others],
            send_sem=rsend.at[0], recv_sem=rrecv.at[p],
            device_id={"branch": sibling}, device_id_type=MESH,
        )

    def own_r(p):
        cut = slice(p * two, (p + 1) * two)
        return pltpu.make_async_copy(
            ox.at[pl.ds(me * cap, cap), cut], orx[p].at[pl.ds(me * cap, cap)], osem.at[p]
        )

    def give_back(p):
        def one(i, c):
            r_copy(p, lax.rem(me + i, n), me).start()
            return c

        lax.fori_loop(1, n, one, 0)
        own_r(p).start()

    own_x.start()
    own_m.start()
    on_lines(0, 1)
    on_lines(1, 1)
    on_lines(2, 1)
    on_lines(3, 1)
    used = n * rlen + width
    if used < tail_n:
        tail[:, used:, :] = jnp.zeros((pairs, tail_n - used, 4 * HD), jnp.bfloat16)
    send_near(0)
    send_far(0)
    on_lines(0, 2)
    on_lines(1, 2)
    on_lines(2, 2)
    on_lines(3, 2)
    send_near(1)
    send_far(1)
    send_near(2)
    send_far(2)
    for j in range(0, 2):
        off_lines(0, j)
    for j in range(0, 2):
        off_lines(1, j)
    for j in range(0, 2):
        off_lines(2, j)
    for j in range(0, 2):
        off_lines(3, j)
    on_lines(0, 3)
    on_lines(1, 3)
    on_lines(2, 3)
    on_lines(3, 3)
    send_near(3)
    send_far(3)
    metas()
    for j in range(2, 4):
        off_lines(0, j)
    tail_keys()
    for j in range(2, 4):
        off_lines(1, j)
    choose(0)
    attend(0)
    give_back(0)
    for j in range(2, 4):
        off_lines(2, j)
    choose(1)
    attend(1)
    give_back(1)
    for j in range(2, 4):
        off_lines(3, j)
    choose(2)
    attend(2)
    give_back(2)
    choose(3)
    attend(3)
    give_back(3)

    for g in range(pairs):
        x_all(g).wait_send()
    m_all().wait_send()
    for g in range(pairs):
        spread(z, g, finish)

    def relayed(t, c):
        for g in range(pairs):
            on_line(t, g, finish, False)
        return c

    lax.fori_loop(1, line, relayed, 0)

    def crossed(t, c):
        for g in range(pairs):
            off_line(t, g, finish, False)
        return c

    if across > 1:
        lax.fori_loop(0, line, crossed, 0)

    for p in range(pairs):
        r_all(p).wait_recv()
        own_r(p).wait()
        for r in range(0, count, some):
            for i in range(some):
                flat[i * two : (i + 1) * two] = orx[p][slot_of[r + i]].astype(jnp.float32)
            for h in range(two):
                at = (p * two + h) * HD
                out_ref[r : r + some, at : at + HD] = flat[
                    pl.ds(h, some, stride=two), :
                ].astype(jnp.bfloat16)
    for p in range(pairs):
        r_all(p).wait_send()


def body(
    across, prompt_k, prompt_v, prompt_mask, shared_kv, shared_len, send_pick,
    unique_q, unique_kv, unique_owner,
):
    n = lax.axis_size("branch")
    rows = unique_q.shape[0]
    cap = 2 * rows // n
    width = n * cap
    res, rlen = shared_kv.shape[:2]
    heads = unique_q.shape[1] // HD
    kvh = unique_kv.shape[1] // (2 * HD)
    pairs = kvh // 2
    plen = prompt_k.shape[1]
    tail_n = -(-(n * rlen + width) // 128) * 128
    qrows = width * GRP
    hbm = pl.BlockSpec(memory_space=pltpu.HBM)
    bf, f32, i32 = jnp.bfloat16, jnp.float32, jnp.int32
    dma = pltpu.SemaphoreType.DMA
    buffers = [
        (unique_q.shape, bf),
        (unique_kv.shape, bf),
        (prompt_k.shape[1:], bf),
        (prompt_v.shape[1:], bf),
        ((max(min(rows, 16) * (heads + 2 * kvh), width * 2 * kvh), HD), f32),
        ((rows, heads + 2 * kvh, HD), bf),
        None,
        ((1, plen), f32),
        ((1, tail_n), f32),
        ((n, 1, HD), i32),
        ((width, heads + 2 * kvh, HD), bf),
        ((width, heads + 2 * kvh, HD), bf),
        ((n, 1, HD), i32),
        ((pairs, tail_n, 4 * HD), bf),
        ((1, tail_n), i32),
        ((width, heads, HD), bf),
    ]
    groups = [((width, 2 * GRP, HD), bf)] * pairs + [((n, res, rlen, 4 * HD), bf)] * pairs
    held = sum(
        math.prod(b[0]) * jnp.dtype(b[1]).itemsize for b in buffers + groups if b is not None
    )
    held += 2 * qrows * (plen + tail_n) * 4
    limit = min(67043328, held * 5 // 4 + 2 * rows * heads * HD + (4 << 20))
    out = pl.pallas_call(
        functools.partial(kernel, n, across, cap, rlen, res, heads),
        out_shape=jax.ShapeDtypeStruct((rows, heads * HD), bf),
        in_specs=[hbm] * 9,
        out_specs=pl.BlockSpec(memory_space=pltpu.VMEM),
        scratch_shapes=[
            pltpu.SMEM((rows,), i32),
            pltpu.SMEM(send_pick.shape, i32),
            pltpu.SMEM(shared_len.shape, i32),
            pltpu.SMEM(prompt_mask.shape, i32),
            pltpu.SMEM((n, 1, HD), i32),
            *[pltpu.SMEM((rows,), i32) if b is None else pltpu.VMEM(*b) for b in buffers],
            dma((9 + pairs,)),
            dma((pairs + 3,)),
            dma((1,)),
            dma((pairs,)),
            dma((1,)),
            dma((1,)),
            dma((1,)),
            dma((n // 2 * pairs,)),
            dma((pairs,)),
            dma((1,)),
            dma((pairs,)),
            *[pltpu.VMEM(*b) for b in groups],
        ],
        compiler_params=pltpu.CompilerParams(
            collective_id=0, has_side_effects=True, vmem_limit_bytes=limit
        ),
    )(
        *[
            pltpu.with_memory_space_constraint(v, pltpu.HBM)
            for v in (
                unique_owner.reshape(rows), send_pick, shared_len, prompt_mask,
                unique_q, unique_kv, shared_kv, prompt_k, prompt_v,
            )
        ]
    )
    return out


def chips_across(mesh):
    devices = mesh.devices.reshape(-1, mesh.shape["branch"])[0]
    try:
        places = [tuple(d.coords) for d in devices[::2]]
    except (AttributeError, TypeError):
        return 1
    return sum(1 for p in places if p[2] == places[0][2])


def solution(mesh):
    spec1, spec2, spec3 = (P(("groups", "branch"), *(None,) * k) for k in range(3))
    in_specs = (spec3, spec3, spec2, spec3, spec1, spec2, spec2, spec2, spec2)
    return jax.shard_map(
        functools.partial(body, chips_across(mesh)),
        mesh=mesh, in_specs=in_specs, out_specs=spec2, check_vma=False,
    )
```

```python
import functools
import math

import jax
import jax.numpy as jnp
from jax import lax
from jax.experimental import pallas as pl
from jax.experimental.pallas import tpu as pltpu
from jax.sharding import PartitionSpec as P

HD = 128
GRP = 8
NEG = -1e30
MESH = pl.DeviceIdType.MESH


def kernel(
    n, across, cap, rlen, res, heads,
    owner_hbm, pick_hbm, len_hbm, mask_hbm, q_hbm, kv_hbm, shared_hbm, pk_hbm, pv_hbm,
    out_ref,
    owner_ref, pick_ref, len_ref, mask_ref, meta_in,
    q_ref, kv_ref, pk, pv, flat, by_row, slot_of, pbias, tbias, meta_ref, mr, tail, kslot,
    lsem, osem, xsend, xrecv, msend, mrecv, gsend, grecv, srecv, rsend, rrecv, rown, *by_group,
):
    me = lax.axis_index("branch")
    kvh = heads // GRP
    pairs = kvh // 2
    orx, ox, gath, xs, xr = (by_group[i * pairs : (i + 1) * pairs] for i in range(5))
    width = n * cap
    rows = width * GRP
    kvw = kvh * HD
    line = n // (2 * across)
    core = lax.rem(me, 2)
    chip = me // 2
    y = lax.rem(chip, across)
    z = chip // across
    sibling = me + 1 - 2 * core
    tail_n = tail.shape[1]
    scale = math.log2(math.e) / math.sqrt(HD)
    two = 2 * GRP
    barrier = pltpu.get_barrier_semaphore()

    def greet(i, c):
        pl.semaphore_signal(
            barrier, inc=1, device_id={"branch": lax.rem(me + i, n)}, device_id_type=MESH
        )
        return c

    lax.fori_loop(1, n, greet, 0)

    gw = 2 * HD

    def load_shared(g, part):
        return pltpu.make_async_copy(
            shared_hbm.at[:, :, pl.ds(part * kvw + g * gw, gw)],
            gath[g].at[me, :, :, pl.ds(part * gw, gw)],
            lsem.at[8 + g],
        )

    copy_q = pltpu.make_async_copy(q_hbm, q_ref, lsem.at[4])
    copy_u = pltpu.make_async_copy(kv_hbm, kv_ref, lsem.at[5])
    copy_k = pltpu.make_async_copy(pk_hbm.at[0], pk, lsem.at[6])
    copy_v = pltpu.make_async_copy(pv_hbm.at[0], pv, lsem.at[7])
    for g in range(pairs):
        for part in range(2):
            load_shared(g, part).start()
    small = [
        pltpu.make_async_copy(src, dst, lsem.at[i])
        for i, (src, dst) in enumerate(
            [(owner_hbm, owner_ref), (pick_hbm, pick_ref), (len_hbm, len_ref), (mask_hbm, mask_ref)]
        )
    ]
    for copy in small:
        copy.start()
    copy_q.start()
    copy_u.start()
    copy_k.start()
    copy_v.start()

    def ship(source, g, target, recv):
        return pltpu.make_async_remote_copy(
            src_ref=gath[g].at[source], dst_ref=gath[g].at[source],
            send_sem=gsend.at[0], recv_sem=recv,
            device_id={"branch": target}, device_id_type=MESH,
        )

    def slot(source, g):
        return grecv.at[(source // 2) * pairs + g]

    def member(zz, yy, cc):
        return (zz * across + yy) * 2 + cc

    def spread(zs, g, act):
        source = member(zs, y, core)
        recv = slot(source, g)

        @pl.when(jnp.logical_and(zs <= z, z + 1 < line))
        def _():
            act(ship(source, g, member(lax.rem(z + 1, line), y, core), recv))

        @pl.when(jnp.logical_and(zs >= z, z >= 1))
        def _():
            act(ship(source, g, member(lax.rem(z + line - 1, line), y, core), recv))

        for d in range(1, across):
            act(ship(source, g, member(z, lax.rem(y + d, across), core), recv))
        act(ship(source, g, sibling, srecv.at[g]))

    def arrived(source, g):
        ship(source, g, sibling, slot(source, g)).wait_recv()

    begin = lambda copy: copy.start()
    finish = lambda copy: copy.wait_send()

    def on_line(t, g, act, waits):
        for up in (0, 1):
            zs = z - t if up == 0 else z + t
            ok = zs >= 0 if up == 0 else zs < line

            @pl.when(ok)
            def _():
                zc = lax.rem(zs + line, line)
                if waits:
                    arrived(member(zc, y, core), g)
                spread(zc, g, act)

    def cross(zs, g, act, waits):
        for d in range(1, across):
            source = member(zs, lax.rem(y + d, across), core)
            if waits:
                arrived(source, g)
            act(ship(source, g, sibling, srecv.at[g]))

    def off_line(t, g, act, waits):
        @pl.when(z - t >= 0)
        def _():
            cross(lax.rem(z - t + line, line), g, act, waits)

        @pl.when(jnp.logical_and(z + t < line, t > 0))
        def _():
            cross(lax.rem(z + t, line), g, act, waits)

    cuts = [0] + [1 + (line - 1) * j // 3 for j in range(4)]

    def own(g):
        spread(z, g, begin)

    def on_lines(g, j):
        def one(t, c):
            on_line(t, g, begin, True)
            return c

        lax.fori_loop(cuts[j], cuts[j + 1], one, 0)

    def off_lines(g, j):
        def one(t, c):
            off_line(t, g, begin, True)
            return c

        if across > 1:
            lax.fori_loop(cuts[j], cuts[j + 1], one, 0)

    def x_copy(g, b, at):
        return pltpu.make_async_remote_copy(
            src_ref=xs[g].at[pl.ds(b * cap, cap)], dst_ref=xr[g].at[pl.ds(at * cap, cap)],
            send_sem=xsend.at[0], recv_sem=xrecv.at[g],
            device_id={"branch": b}, device_id_type=MESH,
        )

    def m_copy(b, at):
        return pltpu.make_async_remote_copy(
            src_ref=meta_ref.at[b], dst_ref=mr.at[at],
            send_sem=msend.at[0], recv_sem=mrecv.at[0],
            device_id={"branch": b}, device_id_type=MESH,
        )

    def each(columns, act):
        def one(i, c):
            for up in (0, 1):
                far = line - 1 - i
                zt = z - far if up == 0 else z + far

                @pl.when(zt >= 0 if up == 0 else zt < line)
                def _():
                    for d in columns:
                        for cc in range(2):
                            act(member(lax.rem(zt + line, line), lax.rem(y + d, across), cc))

            return c

        lax.fori_loop(0, line - 1, one, 0)
        for d in columns:
            for cc in range(2) if d else ():
                act(member(z, lax.rem(y + d, across), cc))
        if 0 in columns:
            act(sibling)

    def send_x(g, columns):
        def to(b):
            x_copy(g, b, me).start()
            if g == 0:
                m_copy(b, me).start()

        each(columns, to)

    others = pl.ds(0, (n - 1) * cap)

    def x_all(g):
        return pltpu.make_async_remote_copy(
            src_ref=xs[g].at[others], dst_ref=xr[g].at[others],
            send_sem=xsend.at[0], recv_sem=xrecv.at[g],
            device_id={"branch": sibling}, device_id_type=MESH,
        )

    def m_all():
        return pltpu.make_async_remote_copy(
            src_ref=meta_ref.at[pl.ds(0, n - 1)], dst_ref=mr.at[pl.ds(0, n - 1)],
            send_sem=msend.at[0], recv_sem=mrecv.at[0],
            device_id={"branch": sibling}, device_id_type=MESH,
        )

    def sib_all(g):
        half = gath[g].at[pl.ds(0, n // 2)]
        return pltpu.make_async_remote_copy(
            src_ref=half, dst_ref=half, send_sem=gsend.at[0], recv_sem=srecv.at[g],
            device_id={"branch": sibling}, device_id_type=MESH,
        )

    def loaded(g):
        mine = gath[g].at[me]
        pltpu.make_async_copy(mine, mine, lsem.at[8 + g]).wait()

    loaded(0)
    pl.semaphore_wait(barrier, n - 1)
    own(0)
    loaded(1)
    own(1)
    loaded(2)
    own(2)
    loaded(3)
    own(3)
    for copy in small:
        copy.wait()
    count = q_ref.shape[0]
    per = heads + 2 * kvh
    some = min(count, 16)

    def number(j, c):
        mine = owner_ref[j]
        rank = lax.fori_loop(
            0, j, lambda i, r: r + jnp.where(owner_ref[i] == mine, 1, 0), jnp.int32(0)
        )
        slot_of[j] = mine * cap + rank
        return c

    lax.fori_loop(0, count, number, 0)
    copy_q.wait()
    copy_u.wait()

    for r in range(0, count, some):
        for h in range(per):
            ref, g = (q_ref, h) if h < heads else (kv_ref, h - heads)
            at = h if h < two else h + 2 * kvh if h < heads else two + g
            flat[pl.ds(at, some, stride=per), :] = ref[
                r : r + some, g * HD : (g + 1) * HD
            ].astype(jnp.float32)
        for i in range(some):
            by_row[r + i] = flat[i * per : (i + 1) * per].astype(jnp.bfloat16)

    lane = lax.broadcasted_iota(jnp.int32, (1, HD), 1)

    def place(b, c):
        def scan(r, found):
            for u in range(some):
                i = r * some + u
                hit = owner_ref[i] == b
                rows_at, seen = found[:cap], found[cap]
                rows_at = [
                    jnp.where(jnp.logical_and(hit, seen == k), i, at)
                    for k, at in enumerate(rows_at)
                ]
                found = (*rows_at, seen + jnp.where(hit, 1, 0))
            return found

        found = lax.fori_loop(0, count // some, scan, (jnp.int32(0),) * (cap + 1))
        pick = pick_ref[0, b]
        length = jnp.int32(0)
        for e in range(res):
            length = jnp.where(pick == e, len_ref[e], length)
        meta_ref[b] = jnp.where(
            lane == 0, pick, jnp.where(lane == 1, length, jnp.where(found[cap] > lane - 2, 1, 0))
        )
        for k in range(cap):
            for g in range(pairs):
                lo = g * two + 2 * kvh if g else 0
                xs[g][b * cap + k] = by_row[found[k], lo : (g + 1) * two + 2 * kvh]
        return c

    lax.fori_loop(0, n, place, 0)
    blocks = mask_ref.shape[1]
    block = pk.shape[0] // blocks
    for g in range(blocks):
        pbias[:, g * block : (g + 1) * block] = jnp.full(
            (1, block), jnp.where(mask_ref[0, g] > 0, 0.0, NEG), jnp.float32
        )

    def part(ref, b):
        return ref.at[pl.ds(b * cap, cap)]

    own_x = [
        pltpu.make_async_copy(part(xs[g], me), part(xr[g], me), osem.at[g]) for g in range(pairs)
    ]
    own_m = pltpu.make_async_copy(meta_ref.at[me], mr.at[me], osem.at[pairs])

    def queries(p):
        both = xr[p][:, :two, :].astype(jnp.float32)
        return [
            both[:, k * GRP : (k + 1) * GRP].reshape(rows, HD).astype(jnp.bfloat16)
            for k in range(2)
        ]

    def scores(q, k):
        return lax.dot_general(q, k, (((1,), (1,)), ((), ())), preferred_element_type=jnp.float32)

    copy_m = pltpu.make_async_copy(mr, meta_in, osem.at[pairs + 1])

    def metas():
        m_all().wait_recv()
        own_m.wait()
        copy_m.start()

    def tail_keys():
        copy_m.wait()
        col = lax.broadcasted_iota(jnp.int32, (1, tail_n), 1)
        owner, at_row = col // rlen, lax.rem(col, rlen)
        some_s = min(n, 16)

        def limits(i, carry):
            length, live = carry
            for u in range(some_s):
                s = i * some_s + u
                length = jnp.where(owner == s, meta_in[s, 0, 1], length)
                for k in range(cap):
                    live = jnp.where(
                        col == n * rlen + s * cap + k, meta_in[s, 0, 2 + k], live
                    )
            return length, live

        zero = jnp.zeros((1, tail_n), jnp.int32)
        length, live = lax.fori_loop(0, n // some_s, limits, (zero, zero))
        shared_ok = jnp.logical_and(col < n * rlen, at_row < length)
        tbias[...] = jnp.where(shared_ok, 0.0, NEG)
        kslot[...] = jnp.where(shared_ok, -1, jnp.where(live > 0, col - n * rlen, width))
        x_all(0).wait_recv()
        own_x[0].wait()
        kv_at = slice(two, two + 2 * kvh)
        flat[: width * 2 * kvh] = (
            xr[0][:, kv_at, :].astype(jnp.float32).reshape(width * 2 * kvh, HD)
        )
        for j in range(2 * kvh):
            at = j % 2 + 2 * (j // kvh)
            tail[j % kvh // 2, n * rlen : n * rlen + width, at * HD : (at + 1) * HD] = flat[
                pl.ds(j, width, stride=2 * kvh), :
            ].astype(jnp.bfloat16)

    row_slot = lax.broadcasted_iota(jnp.int32, (rows, 1), 0) // GRP
    fixed = n * rlen // HD * HD

    def choose(g):
        sib_all(g).wait_recv()
        block = min(n, 16)

        def one(i, c):
            for t in range(0, block, 2):
                two_of = [
                    gath[g][s, jnp.maximum(meta_in[s, 0, 0], 0)].astype(jnp.float32)
                    for s in (i * block + t, i * block + t + 1)
                ]
                at = pl.multiple_of(i * block * rlen + t * rlen, 16)
                tail[g, pl.ds(at, 2 * rlen), :] = jnp.concatenate(two_of, axis=0).astype(
                    jnp.bfloat16
                )
            return c

        lax.fori_loop(0, n // block, one, 0)

    def attend(p):
        if p == 0:
            copy_k.wait()
            copy_v.wait()
        else:
            x_all(p).wait_recv()
            own_x[p].wait()
        done = []
        for k, q in enumerate(queries(p)):
            h = 2 * p + k
            cols = slice(h * HD, (h + 1) * HD)
            keys = tail[p, :, k * HD : (k + 1) * HD]
            values = tail[p, :, (2 + k) * HD : (3 + k) * HD]
            sp = scores(q, pk[:, cols]) * scale + pbias[...]
            st = scores(q, keys) * scale
            sf = st[:, :fixed] + tbias[:, :fixed]
            su = jnp.where(kslot[:, fixed:] <= row_slot, st[:, fixed:], NEG)
            m = jnp.maximum(
                jnp.max(sp, axis=-1, keepdims=True),
                jnp.maximum(
                    jnp.max(sf, axis=-1, keepdims=True), jnp.max(su, axis=-1, keepdims=True)
                ),
            )
            wp = jnp.exp2(sp - m)
            wt = jnp.exp2(jnp.concatenate([sf, su], axis=1) - m)
            total = jnp.sum(wp, axis=-1, keepdims=True) + jnp.sum(wt, axis=-1, keepdims=True)
            mixed = jnp.dot(
                wp.astype(jnp.bfloat16), pv[:, cols], preferred_element_type=jnp.float32
            ) + jnp.dot(wt.astype(jnp.bfloat16), values, preferred_element_type=jnp.float32)
            done.append((mixed / total).reshape(width, GRP, HD))
        ox[p][...] = jnp.concatenate(done, axis=1).astype(jnp.bfloat16)

    def r_copy(p, b, at):
        return pltpu.make_async_remote_copy(
            src_ref=ox[p].at[pl.ds(b * cap, cap)], dst_ref=orx[p].at[pl.ds(at * cap, cap)],
            send_sem=rsend.at[0], recv_sem=rrecv.at[p],
            device_id={"branch": b}, device_id_type=MESH,
        )

    def r_all(p):
        return pltpu.make_async_remote_copy(
            src_ref=ox[p].at[others], dst_ref=orx[p].at[others],
            send_sem=rsend.at[0], recv_sem=rrecv.at[p],
            device_id={"branch": sibling}, device_id_type=MESH,
        )

    def own_r(p):
        return pltpu.make_async_copy(part(ox[p], me), part(orx[p], me), rown.at[p])

    def give_back(p):
        each(range(across), lambda b: r_copy(p, b, me).start())
        own_r(p).start()

    for copy in own_x:
        copy.start()
    own_m.start()
    send_x(0, range(across))
    on_lines(0, 1)
    on_lines(1, 1)
    on_lines(2, 1)
    on_lines(3, 1)
    used = n * rlen + width
    if used < tail_n:
        tail[:, used:, :] = jnp.zeros((pairs, tail_n - used, 4 * HD), jnp.bfloat16)
    on_lines(0, 2)
    on_lines(1, 2)
    send_x(1, range(across))
    on_lines(2, 2)
    on_lines(3, 2)
    for j in range(0, 2):
        off_lines(0, j)
    for j in range(0, 2):
        off_lines(1, j)
    for j in range(0, 2):
        off_lines(2, j)
    for j in range(0, 2):
        off_lines(3, j)
    on_lines(0, 3)
    send_x(2, range(across))
    on_lines(1, 3)
    on_lines(2, 3)
    on_lines(3, 3)
    send_x(3, range(across))
    metas()
    for j in range(2, 4):
        off_lines(0, j)
    tail_keys()
    for j in range(2, 4):
        off_lines(1, j)
    choose(0)
    attend(0)
    give_back(0)
    for j in range(2, 4):
        off_lines(2, j)
    choose(1)
    attend(1)
    give_back(1)
    for j in range(2, 4):
        off_lines(3, j)
    choose(2)
    attend(2)
    give_back(2)
    choose(3)
    attend(3)
    give_back(3)

    for g in range(pairs):
        x_all(g).wait_send()
    m_all().wait_send()
    for g in range(pairs):
        spread(z, g, finish)

    def relayed(t, c):
        for g in range(pairs):
            on_line(t, g, finish, False)
        return c

    lax.fori_loop(1, line, relayed, 0)

    def crossed(t, c):
        for g in range(pairs):
            off_line(t, g, finish, False)
        return c

    if across > 1:
        lax.fori_loop(0, line, crossed, 0)

    for p in range(pairs):
        r_all(p).wait_recv()
        own_r(p).wait()
        for r in range(0, count, some):
            for i in range(some):
                flat[i * two : (i + 1) * two] = orx[p][slot_of[r + i]].astype(jnp.float32)
            for h in range(two):
                at = (p * two + h) * HD
                out_ref[r : r + some, at : at + HD] = flat[
                    pl.ds(h, some, stride=two), :
                ].astype(jnp.bfloat16)
    for p in range(pairs):
        r_all(p).wait_send()


def body(
    across, prompt_k, prompt_v, prompt_mask, shared_kv, shared_len, send_pick,
    unique_q, unique_kv, unique_owner,
):
    n = lax.axis_size("branch")
    rows = unique_q.shape[0]
    cap = 2 * rows // n
    width = n * cap
    res, rlen = shared_kv.shape[:2]
    heads = unique_q.shape[1] // HD
    kvh = unique_kv.shape[1] // (2 * HD)
    pairs = kvh // 2
    plen = prompt_k.shape[1]
    tail_n = -(-(n * rlen + width) // 128) * 128
    qrows = width * GRP
    hbm = pl.BlockSpec(memory_space=pltpu.HBM)
    bf, f32, i32 = jnp.bfloat16, jnp.float32, jnp.int32
    dma = pltpu.SemaphoreType.DMA
    buffers = [
        (unique_q.shape, bf),
        (unique_kv.shape, bf),
        (prompt_k.shape[1:], bf),
        (prompt_v.shape[1:], bf),
        ((max(min(rows, 16) * (heads + 2 * kvh), width * 2 * kvh), HD), f32),
        ((rows, heads + 2 * kvh, HD), bf),
        None,
        ((1, plen), f32),
        ((1, tail_n), f32),
        ((n, 1, HD), i32),
        ((n, 1, HD), i32),
        ((pairs, tail_n, 4 * HD), bf),
        ((1, tail_n), i32),
    ]
    groups = [((width, 2 * GRP, HD), bf)] * (2 * pairs) + [((n, res, rlen, 4 * HD), bf)] * pairs
    halves = [((width, 2 * GRP + (0 if g else 2 * kvh), HD), bf) for g in range(pairs)]
    groups += halves * 2
    held = sum(
        math.prod(b[0]) * jnp.dtype(b[1]).itemsize for b in buffers + groups if b is not None
    )
    held += 2 * qrows * (plen + tail_n) * 4
    limit = min(67043328, held * 5 // 4 + 2 * rows * heads * HD + (4 << 20))
    out = pl.pallas_call(
        functools.partial(kernel, n, across, cap, rlen, res, heads),
        out_shape=jax.ShapeDtypeStruct((rows, heads * HD), bf),
        in_specs=[hbm] * 9,
        out_specs=pl.BlockSpec(memory_space=pltpu.VMEM),
        scratch_shapes=[
            pltpu.SMEM((rows,), i32),
            pltpu.SMEM(send_pick.shape, i32),
            pltpu.SMEM(shared_len.shape, i32),
            pltpu.SMEM(prompt_mask.shape, i32),
            pltpu.SMEM((n, 1, HD), i32),
            *[pltpu.SMEM((rows,), i32) if b is None else pltpu.VMEM(*b) for b in buffers],
            dma((8 + pairs,)),
            dma((pairs + 2,)),
            dma((1,)),
            dma((pairs,)),
            dma((1,)),
            dma((1,)),
            dma((1,)),
            dma((n // 2 * pairs,)),
            dma((pairs,)),
            dma((1,)),
            dma((pairs,)),
            dma((pairs,)),
            *[pltpu.VMEM(*b) for b in groups],
        ],
        compiler_params=pltpu.CompilerParams(
            collective_id=0, has_side_effects=True, vmem_limit_bytes=limit
        ),
    )(
        *[
            pltpu.with_memory_space_constraint(v, pltpu.HBM)
            for v in (
                unique_owner.reshape(rows), send_pick, shared_len, prompt_mask,
                unique_q, unique_kv, shared_kv, prompt_k, prompt_v,
            )
        ]
    )
    return out


def chips_across(mesh):
    devices = mesh.devices.reshape(-1, mesh.shape["branch"])[0]
    try:
        places = [tuple(d.coords) for d in devices[::2]]
    except (AttributeError, TypeError):
        return 1
    return sum(1 for p in places if p[2] == places[0][2])


def solution(mesh):
    spec1, spec2, spec3 = (P(("groups", "branch"), *(None,) * k) for k in range(3))
    in_specs = (spec3, spec3, spec2, spec3, spec1, spec2, spec2, spec2, spec2)
    return jax.shard_map(
        functools.partial(body, chips_across(mesh)),
        mesh=mesh, in_specs=in_specs, out_specs=spec2, check_vma=False,
    )
```

```python
import functools
import math

import jax
import jax.numpy as jnp
from jax import lax
from jax.experimental import pallas as pl
from jax.experimental.pallas import tpu as pltpu
from jax.sharding import PartitionSpec as P

HD = 128
GRP = 8
NEG = -1e30
MESH = pl.DeviceIdType.MESH


def kernel(
    n, across, cap, rlen, res, heads,
    owner_hbm, pick_hbm, len_hbm, mask_hbm, q_hbm, kv_hbm, shared_hbm, pk_hbm, pv_hbm,
    out_ref,
    owner_ref, pick_ref, len_ref, mask_ref, meta_in,
    q_ref, kv_ref, pk, pv, flat, by_row, slot_of, pbias, tbias, meta_ref, mr, tail, kslot,
    lsem, osem, xsend, xrecv, msend, mrecv, gsend, grecv, srecv, rsend, rrecv, *by_group,
):
    me = lax.axis_index("branch")
    kvh = heads // GRP
    pairs = kvh // 2
    orx, ox, gath, xs, xr = (by_group[i * pairs : (i + 1) * pairs] for i in range(5))
    width = n * cap
    rows = width * GRP
    kvw = kvh * HD
    line = n // (2 * across)
    core = lax.rem(me, 2)
    chip = me // 2
    y = lax.rem(chip, across)
    z = chip // across
    sibling = me + 1 - 2 * core
    tail_n = tail.shape[1]
    scale = math.log2(math.e) / math.sqrt(HD)
    two = 2 * GRP
    barrier = pltpu.get_barrier_semaphore()

    def greet(i, c):
        pl.semaphore_signal(
            barrier, inc=1, device_id={"branch": lax.rem(me + i, n)}, device_id_type=MESH
        )
        return c

    lax.fori_loop(1, n, greet, 0)

    gw = 2 * HD

    def load_shared(g, part):
        return pltpu.make_async_copy(
            shared_hbm.at[:, :, pl.ds(part * kvw + g * gw, gw)],
            gath[g].at[me, :, :, pl.ds(part * gw, gw)],
            lsem.at[8 + g],
        )

    copy_q = pltpu.make_async_copy(q_hbm, q_ref, lsem.at[4])
    copy_u = pltpu.make_async_copy(kv_hbm, kv_ref, lsem.at[5])
    copy_k = pltpu.make_async_copy(pk_hbm.at[0], pk, lsem.at[6])
    copy_v = pltpu.make_async_copy(pv_hbm.at[0], pv, lsem.at[7])
    for g in range(pairs):
        for part in range(2):
            load_shared(g, part).start()
    small = [
        pltpu.make_async_copy(src, dst, lsem.at[i])
        for i, (src, dst) in enumerate(
            [(owner_hbm, owner_ref), (pick_hbm, pick_ref), (len_hbm, len_ref), (mask_hbm, mask_ref)]
        )
    ]
    for copy in small:
        copy.start()
    copy_q.start()
    copy_u.start()
    copy_k.start()
    copy_v.start()

    def ship(source, g, target, recv):
        return pltpu.make_async_remote_copy(
            src_ref=gath[g].at[source], dst_ref=gath[g].at[source],
            send_sem=gsend.at[0], recv_sem=recv,
            device_id={"branch": target}, device_id_type=MESH,
        )

    def slot(source, g):
        return grecv.at[(source // 2) * pairs + g]

    def member(zz, yy, cc):
        return (zz * across + yy) * 2 + cc

    def spread(zs, g, act):
        source = member(zs, y, core)
        recv = slot(source, g)

        @pl.when(jnp.logical_and(zs <= z, z + 1 < line))
        def _():
            act(ship(source, g, member(lax.rem(z + 1, line), y, core), recv))

        @pl.when(jnp.logical_and(zs >= z, z >= 1))
        def _():
            act(ship(source, g, member(lax.rem(z + line - 1, line), y, core), recv))

        for d in range(1, across):
            act(ship(source, g, member(z, lax.rem(y + d, across), core), recv))
        act(ship(source, g, sibling, srecv.at[g]))

    def arrived(source, g):
        ship(source, g, sibling, slot(source, g)).wait_recv()

    begin = lambda copy: copy.start()
    finish = lambda copy: copy.wait_send()

    def on_line(t, g, act, waits):
        for up in (0, 1):
            zs = z - t if up == 0 else z + t
            ok = zs >= 0 if up == 0 else zs < line

            @pl.when(ok)
            def _():
                zc = lax.rem(zs + line, line)
                if waits:
                    arrived(member(zc, y, core), g)
                spread(zc, g, act)

    def cross(zs, g, act, waits):
        for d in range(1, across):
            source = member(zs, lax.rem(y + d, across), core)
            if waits:
                arrived(source, g)
            act(ship(source, g, sibling, srecv.at[g]))

    def off_line(t, g, act, waits):
        @pl.when(z - t >= 0)
        def _():
            cross(lax.rem(z - t + line, line), g, act, waits)

        @pl.when(jnp.logical_and(z + t < line, t > 0))
        def _():
            cross(lax.rem(z + t, line), g, act, waits)

    cuts = [0] + [1 + (line - 1) * j // 3 for j in range(4)]

    def own(g):
        spread(z, g, begin)

    def on_lines(g, j):
        def one(t, c):
            on_line(t, g, begin, True)
            return c

        lax.fori_loop(cuts[j], cuts[j + 1], one, 0)

    def off_lines(g, j):
        def one(t, c):
            off_line(t, g, begin, True)
            return c

        if across > 1:
            lax.fori_loop(cuts[j], cuts[j + 1], one, 0)

    def x_copy(g, b, at):
        return pltpu.make_async_remote_copy(
            src_ref=xs[g].at[pl.ds(b * cap, cap)], dst_ref=xr[g].at[pl.ds(at * cap, cap)],
            send_sem=xsend.at[0], recv_sem=xrecv.at[g],
            device_id={"branch": b}, device_id_type=MESH,
        )

    def m_copy(b, at):
        return pltpu.make_async_remote_copy(
            src_ref=meta_ref.at[b], dst_ref=mr.at[at],
            send_sem=msend.at[0], recv_sem=mrecv.at[0],
            device_id={"branch": b}, device_id_type=MESH,
        )

    def each(columns, act):
        def one(i, c):
            for up in (0, 1):
                far = line - 1 - i
                zt = z - far if up == 0 else z + far

                @pl.when(zt >= 0 if up == 0 else zt < line)
                def _():
                    for d in columns:
                        for cc in range(2):
                            act(member(lax.rem(zt + line, line), lax.rem(y + d, across), cc))

            return c

        lax.fori_loop(0, line - 1, one, 0)
        for d in columns:
            for cc in range(2) if d else ():
                act(member(z, lax.rem(y + d, across), cc))
        if 0 in columns:
            act(sibling)

    def send_x(g, columns):
        def to(b):
            x_copy(g, b, me).start()
            if g == 0:
                m_copy(b, me).start()

        each(columns, to)

    others = pl.ds(0, (n - 1) * cap)

    def x_all(g):
        return pltpu.make_async_remote_copy(
            src_ref=xs[g].at[others], dst_ref=xr[g].at[others],
            send_sem=xsend.at[0], recv_sem=xrecv.at[g],
            device_id={"branch": sibling}, device_id_type=MESH,
        )

    def m_all():
        return pltpu.make_async_remote_copy(
            src_ref=meta_ref.at[pl.ds(0, n - 1)], dst_ref=mr.at[pl.ds(0, n - 1)],
            send_sem=msend.at[0], recv_sem=mrecv.at[0],
            device_id={"branch": sibling}, device_id_type=MESH,
        )

    def sib_all(g):
        half = gath[g].at[pl.ds(0, n // 2)]
        return pltpu.make_async_remote_copy(
            src_ref=half, dst_ref=half, send_sem=gsend.at[0], recv_sem=srecv.at[g],
            device_id={"branch": sibling}, device_id_type=MESH,
        )

    def loaded(g):
        mine = gath[g].at[me]
        pltpu.make_async_copy(mine, mine, lsem.at[8 + g]).wait()

    loaded(0)
    pl.semaphore_wait(barrier, n - 1)
    own(0)
    loaded(1)
    own(1)
    loaded(2)
    own(2)
    loaded(3)
    own(3)
    for copy in small:
        copy.wait()
    count = q_ref.shape[0]
    per = heads + 2 * kvh
    some = min(count, 16)

    def number(j, c):
        mine = owner_ref[j]
        rank = lax.fori_loop(
            0, j, lambda i, r: r + jnp.where(owner_ref[i] == mine, 1, 0), jnp.int32(0)
        )
        slot_of[j] = mine * cap + rank
        return c

    lax.fori_loop(0, count, number, 0)
    copy_q.wait()
    copy_u.wait()

    for r in range(0, count, some):
        for h in range(per):
            ref, g = (q_ref, h) if h < heads else (kv_ref, h - heads)
            at = h if h < two else h + 2 * kvh if h < heads else two + g
            flat[pl.ds(at, some, stride=per), :] = ref[
                r : r + some, g * HD : (g + 1) * HD
            ].astype(jnp.float32)
        for i in range(some):
            by_row[r + i] = flat[i * per : (i + 1) * per].astype(jnp.bfloat16)

    lane = lax.broadcasted_iota(jnp.int32, (1, HD), 1)

    def place(b, c):
        def scan(r, found):
            for u in range(some):
                i = r * some + u
                hit = owner_ref[i] == b
                rows_at, seen = found[:cap], found[cap]
                rows_at = [
                    jnp.where(jnp.logical_and(hit, seen == k), i, at)
                    for k, at in enumerate(rows_at)
                ]
                found = (*rows_at, seen + jnp.where(hit, 1, 0))
            return found

        found = lax.fori_loop(0, count // some, scan, (jnp.int32(0),) * (cap + 1))
        pick = pick_ref[0, b]
        length = jnp.int32(0)
        for e in range(res):
            length = jnp.where(pick == e, len_ref[e], length)
        meta_ref[b] = jnp.where(
            lane == 0, pick, jnp.where(lane == 1, length, jnp.where(found[cap] > lane - 2, 1, 0))
        )
        for k in range(cap):
            for g in range(pairs):
                lo = g * two + 2 * kvh if g else 0
                xs[g][b * cap + k] = by_row[found[k], lo : (g + 1) * two + 2 * kvh]
        return c

    lax.fori_loop(0, n, place, 0)
    blocks = mask_ref.shape[1]
    block = pk.shape[0] // blocks
    for g in range(blocks):
        pbias[:, g * block : (g + 1) * block] = jnp.full(
            (1, block), jnp.where(mask_ref[0, g] > 0, 0.0, NEG), jnp.float32
        )

    def queries(p):
        both = xr[p][:, :two, :].astype(jnp.float32)
        return [
            both[:, k * GRP : (k + 1) * GRP].reshape(rows, HD).astype(jnp.bfloat16)
            for k in range(2)
        ]

    def scores(q, k):
        return lax.dot_general(q, k, (((1,), (1,)), ((), ())), preferred_element_type=jnp.float32)

    copy_m = pltpu.make_async_copy(mr, meta_in, osem.at[0])

    def metas():
        m_all().wait_recv()
        copy_m.start()

    def tail_keys():
        copy_m.wait()
        col = lax.broadcasted_iota(jnp.int32, (1, tail_n), 1)
        owner, at_row = col // rlen, lax.rem(col, rlen)
        some_s = min(n, 16)

        def limits(i, carry):
            length, live = carry
            for u in range(some_s):
                s = i * some_s + u
                length = jnp.where(owner == s, meta_in[s, 0, 1], length)
                for k in range(cap):
                    live = jnp.where(
                        col == n * rlen + s * cap + k, meta_in[s, 0, 2 + k], live
                    )
            return length, live

        zero = jnp.zeros((1, tail_n), jnp.int32)
        length, live = lax.fori_loop(0, n // some_s, limits, (zero, zero))
        shared_ok = jnp.logical_and(col < n * rlen, at_row < length)
        tbias[...] = jnp.where(shared_ok, 0.0, NEG)
        kslot[...] = jnp.where(shared_ok, -1, jnp.where(live > 0, col - n * rlen, width))
        x_all(0).wait_recv()
        kv_at = slice(two, two + 2 * kvh)
        flat[: width * 2 * kvh] = (
            xr[0][:, kv_at, :].astype(jnp.float32).reshape(width * 2 * kvh, HD)
        )
        for j in range(2 * kvh):
            at = j % 2 + 2 * (j // kvh)
            tail[j % kvh // 2, n * rlen : n * rlen + width, at * HD : (at + 1) * HD] = flat[
                pl.ds(j, width, stride=2 * kvh), :
            ].astype(jnp.bfloat16)

    row_slot = lax.broadcasted_iota(jnp.int32, (rows, 1), 0) // GRP
    fixed = n * rlen // HD * HD

    def choose(g):
        sib_all(g).wait_recv()
        block = min(n, 16)

        def one(i, c):
            for t in range(0, block, 2):
                two_of = [
                    gath[g][s, jnp.maximum(meta_in[s, 0, 0], 0)].astype(jnp.float32)
                    for s in (i * block + t, i * block + t + 1)
                ]
                at = pl.multiple_of(i * block * rlen + t * rlen, 16)
                tail[g, pl.ds(at, 2 * rlen), :] = jnp.concatenate(two_of, axis=0).astype(
                    jnp.bfloat16
                )
            return c

        lax.fori_loop(0, n // block, one, 0)

    def attend(p):
        if p == 0:
            copy_k.wait()
            copy_v.wait()
        else:
            x_all(p).wait_recv()
        done = []
        for k, q in enumerate(queries(p)):
            h = 2 * p + k
            cols = slice(h * HD, (h + 1) * HD)
            keys = tail[p, :, k * HD : (k + 1) * HD]
            values = tail[p, :, (2 + k) * HD : (3 + k) * HD]
            sp = scores(q, pk[:, cols]) * scale + pbias[...]
            st = scores(q, keys) * scale
            sf = st[:, :fixed] + tbias[:, :fixed]
            su = jnp.where(kslot[:, fixed:] <= row_slot, st[:, fixed:], NEG)
            m = jnp.maximum(
                jnp.max(sp, axis=-1, keepdims=True),
                jnp.maximum(
                    jnp.max(sf, axis=-1, keepdims=True), jnp.max(su, axis=-1, keepdims=True)
                ),
            )
            wp = jnp.exp2(sp - m)
            wt = jnp.exp2(jnp.concatenate([sf, su], axis=1) - m)
            total = jnp.sum(wp, axis=-1, keepdims=True) + jnp.sum(wt, axis=-1, keepdims=True)
            mixed = jnp.dot(
                wp.astype(jnp.bfloat16), pv[:, cols], preferred_element_type=jnp.float32
            ) + jnp.dot(wt.astype(jnp.bfloat16), values, preferred_element_type=jnp.float32)
            done.append((mixed / total).reshape(width, GRP, HD))
        ox[p][...] = jnp.concatenate(done, axis=1).astype(jnp.bfloat16)

    def r_copy(p, b, at):
        return pltpu.make_async_remote_copy(
            src_ref=ox[p].at[pl.ds(b * cap, cap)], dst_ref=orx[p].at[pl.ds(at * cap, cap)],
            send_sem=rsend.at[0], recv_sem=rrecv.at[p],
            device_id={"branch": b}, device_id_type=MESH,
        )

    def r_all(p):
        return pltpu.make_async_remote_copy(
            src_ref=ox[p].at[others], dst_ref=orx[p].at[others],
            send_sem=rsend.at[0], recv_sem=rrecv.at[p],
            device_id={"branch": sibling}, device_id_type=MESH,
        )

    def give_back(p):
        each(range(across), lambda b: r_copy(p, b, me).start())
        orx[p][mine] = ox[p][mine]

    mine = pl.ds(me * cap, cap)
    for g in range(pairs):
        xr[g][mine] = xs[g][mine]
    mr[me] = meta_ref[me]
    send_x(0, range(across))
    on_lines(0, 1)
    on_lines(1, 1)
    on_lines(2, 1)
    on_lines(3, 1)
    used = n * rlen + width
    if used < tail_n:
        tail[:, used:, :] = jnp.zeros((pairs, tail_n - used, 4 * HD), jnp.bfloat16)
    on_lines(0, 2)
    on_lines(1, 2)
    send_x(1, range(across))
    on_lines(2, 2)
    on_lines(3, 2)
    for j in range(0, 2):
        off_lines(0, j)
    for j in range(0, 2):
        off_lines(1, j)
    for j in range(0, 2):
        off_lines(2, j)
    for j in range(0, 2):
        off_lines(3, j)
    on_lines(0, 3)
    send_x(2, range(across))
    on_lines(1, 3)
    on_lines(2, 3)
    on_lines(3, 3)
    send_x(3, range(across))
    metas()
    for j in range(2, 4):
        off_lines(0, j)
    tail_keys()
    for j in range(2, 4):
        off_lines(1, j)
    choose(0)
    attend(0)
    give_back(0)
    for j in range(2, 4):
        off_lines(2, j)
    choose(1)
    attend(1)
    give_back(1)
    for j in range(2, 4):
        off_lines(3, j)
    choose(2)
    attend(2)
    give_back(2)
    choose(3)
    attend(3)
    give_back(3)

    for g in range(pairs):
        x_all(g).wait_send()
    m_all().wait_send()
    for g in range(pairs):
        spread(z, g, finish)

    def relayed(t, c):
        for g in range(pairs):
            on_line(t, g, finish, False)
        return c

    lax.fori_loop(1, line, relayed, 0)

    def crossed(t, c):
        for g in range(pairs):
            off_line(t, g, finish, False)
        return c

    if across > 1:
        lax.fori_loop(0, line, crossed, 0)

    for p in range(pairs):
        r_all(p).wait_recv()
        for r in range(0, count, some):
            for i in range(some):
                flat[i * two : (i + 1) * two] = orx[p][slot_of[r + i]].astype(jnp.float32)
            for h in range(two):
                at = (p * two + h) * HD
                out_ref[r : r + some, at : at + HD] = flat[
                    pl.ds(h, some, stride=two), :
                ].astype(jnp.bfloat16)
    for p in range(pairs):
        r_all(p).wait_send()


def body(
    across, prompt_k, prompt_v, prompt_mask, shared_kv, shared_len, send_pick,
    unique_q, unique_kv, unique_owner,
):
    n = lax.axis_size("branch")
    rows = unique_q.shape[0]
    cap = 2 * rows // n
    width = n * cap
    res, rlen = shared_kv.shape[:2]
    heads = unique_q.shape[1] // HD
    kvh = unique_kv.shape[1] // (2 * HD)
    pairs = kvh // 2
    plen = prompt_k.shape[1]
    tail_n = -(-(n * rlen + width) // 128) * 128
    qrows = width * GRP
    hbm = pl.BlockSpec(memory_space=pltpu.HBM)
    bf, f32, i32 = jnp.bfloat16, jnp.float32, jnp.int32
    dma = pltpu.SemaphoreType.DMA
    buffers = [
        (unique_q.shape, bf),
        (unique_kv.shape, bf),
        (prompt_k.shape[1:], bf),
        (prompt_v.shape[1:], bf),
        ((max(min(rows, 16) * (heads + 2 * kvh), width * 2 * kvh), HD), f32),
        ((rows, heads + 2 * kvh, HD), bf),
        None,
        ((1, plen), f32),
        ((1, tail_n), f32),
        ((n, 1, HD), i32),
        ((n, 1, HD), i32),
        ((pairs, tail_n, 4 * HD), bf),
        ((1, tail_n), i32),
    ]
    groups = [((width, 2 * GRP, HD), bf)] * (2 * pairs) + [((n, res, rlen, 4 * HD), bf)] * pairs
    halves = [((width, 2 * GRP + (0 if g else 2 * kvh), HD), bf) for g in range(pairs)]
    groups += halves * 2
    held = sum(
        math.prod(b[0]) * jnp.dtype(b[1]).itemsize for b in buffers + groups if b is not None
    )
    held += 2 * qrows * (plen + tail_n) * 4
    limit = min(67043328, held * 5 // 4 + 2 * rows * heads * HD + (4 << 20))
    out = pl.pallas_call(
        functools.partial(kernel, n, across, cap, rlen, res, heads),
        out_shape=jax.ShapeDtypeStruct((rows, heads * HD), bf),
        in_specs=[hbm] * 9,
        out_specs=pl.BlockSpec(memory_space=pltpu.VMEM),
        scratch_shapes=[
            pltpu.SMEM((rows,), i32),
            pltpu.SMEM(send_pick.shape, i32),
            pltpu.SMEM(shared_len.shape, i32),
            pltpu.SMEM(prompt_mask.shape, i32),
            pltpu.SMEM((n, 1, HD), i32),
            *[pltpu.SMEM((rows,), i32) if b is None else pltpu.VMEM(*b) for b in buffers],
            dma((8 + pairs,)),
            dma((1,)),
            dma((1,)),
            dma((pairs,)),
            dma((1,)),
            dma((1,)),
            dma((1,)),
            dma((n // 2 * pairs,)),
            dma((pairs,)),
            dma((1,)),
            dma((pairs,)),
            *[pltpu.VMEM(*b) for b in groups],
        ],
        compiler_params=pltpu.CompilerParams(
            collective_id=0, has_side_effects=True, vmem_limit_bytes=limit
        ),
    )(
        *[
            pltpu.with_memory_space_constraint(v, pltpu.HBM)
            for v in (
                unique_owner.reshape(rows), send_pick, shared_len, prompt_mask,
                unique_q, unique_kv, shared_kv, prompt_k, prompt_v,
            )
        ]
    )
    return out


def chips_across(mesh):
    devices = mesh.devices.reshape(-1, mesh.shape["branch"])[0]
    try:
        places = [tuple(d.coords) for d in devices[::2]]
    except (AttributeError, TypeError):
        return 1
    return sum(1 for p in places if p[2] == places[0][2])


def solution(mesh):
    spec1, spec2, spec3 = (P(("groups", "branch"), *(None,) * k) for k in range(3))
    in_specs = (spec3, spec3, spec2, spec3, spec1, spec2, spec2, spec2, spec2)
    return jax.shard_map(
        functools.partial(body, chips_across(mesh)),
        mesh=mesh, in_specs=in_specs, out_specs=spec2, check_vma=False,
    )
```
